32 devices in a mesh: row: 8 (over z, y), col: 4 (over x, core).
Axes of the slice: x: 2, y: 2, z: 4, core: 2. Of those that a mesh axis runs over, the one named last changes fastest.
Arguments:
- source: float32 [16384, 512], P(('row', 'col')), may hold values from -1.3 to 1.3
- context: float32 [16384, 512], P(('row', 'col')), may hold values from -1.3 to 1.3
- pair_counts: int32 [4, 16384, 512], P(None, ('row', 'col')), may hold values from 0 to 4
- partner_masks: int32 [4], replicated, may hold values from 1 to 7, as said below
Outputs:
- source_out: float32 [16384, 512], P(('row', 'col'))
- context_out: float32 [16384, 512], P(('row', 'col'))
The draws below stay inside these ranges and needn't reach their ends.
Inputs may be any that keep to these rules, and one draw needn't show every extreme that they name: `partner_masks`: entry k is the offset of round k: for even k it is below 8, for odd k below 4; never zero.
All inputs are finite; a program needn't handle non-finite values.
Results may differ from the reference program's by a relative error of at most 0.0019.
Values sent between devices are 32-bit elements; how exact they have to be, the bound alone decides.
No kernel may reach another device: no remote copies, remote signals or barrier semaphores. Data moves between devices by JAX's collectives and lax.ppermute only.
A program may use at most 128 MiB of HBM per device.

```python
import jax
import jax.numpy as jnp
from jax import lax

D = 512
SRC_DEV = 512
CTX_DEV = 512
ROUNDS = 4
SOURCES = 16384
CONTEXTS = 16384
N_ROW = 8
N_COL = 4


def draw_source(key, part):
    entry_key = jax.random.fold_in(key, 11)
    values = jnp.clip(jax.random.normal(entry_key, (SOURCES, D), jnp.float32), -6.0, 6.0) * 0.21
    return values.astype(jnp.float32)


def draw_context(key, part):
    entry_key = jax.random.fold_in(key, 12)
    values = jnp.clip(jax.random.normal(entry_key, (CONTEXTS, D), jnp.float32), -6.0, 6.0) * 0.21
    return values.astype(jnp.float32)


def draw_partner_masks(key, part):
    turns = jnp.arange(ROUNDS, dtype=jnp.int32)
    limits = jnp.where(turns % 2 == 0, N_ROW, N_COL).astype(jnp.int32)
    raw_bits = jax.random.randint(jax.random.fold_in(key, 13), (ROUNDS,), 0, 1048576, jnp.int32)
    offsets = (1 + raw_bits % (limits - 1)).astype(jnp.int32)
    biggest = jnp.max(limits)
    pick_bits = jax.random.randint(jax.random.fold_in(key, 14), (ROUNDS,), 0, 1048576, jnp.int32)
    scores = jnp.where(limits == biggest, pick_bits * ROUNDS + turns, -1).astype(jnp.int32)
    chosen = lax.top_k(scores, 1)[1][0].astype(jnp.int32)
    offsets = jnp.where(turns == chosen, limits - 1, offsets)
    return offsets.astype(jnp.int32)


def with_ends(result, own_key, least, high):
    longest = result.shape.index(max(result.shape))
    spots = []
    for shift in (0, 1):
        where = [jax.random.randint(jax.random.fold_in(own_key, axis), (), 0, length) for axis, length in enumerate(result.shape)]
        where[longest] = (where[longest] + shift) % result.shape[longest]
        spots.append(tuple(where))
    return result.at[spots[0]].set(least).at[spots[1]].set(high)


def setup_inputs(seed: int = 0) -> dict:
    seeds = jax.random.split(jax.random.key(seed), 5)
    return {
        "source": draw_source(jax.random.fold_in(seeds[4], 71), 0),
        "context": draw_context(jax.random.fold_in(seeds[4], 71), 0),
        "pair_counts": with_ends(jax.random.randint(seeds[2], (ROUNDS, SOURCES, CTX_DEV), 0, 5), jax.random.fold_in(seeds[2], 1), 0, 4).astype(jnp.int32),
        "partner_masks": draw_partner_masks(jax.random.fold_in(seeds[4], 71), 0),
    }


LEARN_RATE = 0.05
NEG_WEIGHT = 1.0
EPSILON = 1e-06

def rounded(values):
    half = lax.optimization_barrier(values.astype(jnp.bfloat16))
    return half.astype(jnp.float32)

def normalized(param, grad):
    scale = lax.rsqrt(lax.optimization_barrier(jnp.mean(grad * grad, axis=1, keepdims=True)) + EPSILON)
    return param - LEARN_RATE * grad * scale

def train_pair(operands):
    src_block, ctx_block, tile = operands
    src_low = rounded(src_block)
    ctx_low = rounded(ctx_block)
    scores = jnp.dot(src_low, ctx_low.T, preferred_element_type=jnp.float32, precision=lax.Precision.HIGHEST)
    weight = tile.astype(jnp.float32)
    coef = rounded((weight + NEG_WEIGHT) * jax.nn.sigmoid(scores) - weight)
    grad_src = jnp.dot(coef, ctx_low, preferred_element_type=jnp.float32, precision=lax.Precision.HIGHEST)
    grad_ctx = jnp.dot(coef.T, src_low, preferred_element_type=jnp.float32, precision=lax.Precision.HIGHEST)
    return (normalized(src_block, grad_src), normalized(ctx_block, grad_ctx))

def reference(source, context, pair_counts, partner_masks):
    blocks = N_ROW * N_COL
    sources = source.reshape(blocks, SRC_DEV, D)
    contexts = context.reshape(blocks, CTX_DEV, D)
    row_ids = jnp.repeat(jnp.arange(N_ROW, dtype=jnp.int32), N_COL)
    col_ids = jnp.tile(jnp.arange(N_COL, dtype=jnp.int32), N_ROW)
    row_total = jnp.zeros((), jnp.int32)
    col_total = jnp.zeros((), jnp.int32)
    for turn in range(ROUNDS):
        if turn % 2 == 0:
            row_total = (row_total + partner_masks[turn].astype(jnp.int32)) % N_ROW
        else:
            col_total = (col_total + partner_masks[turn].astype(jnp.int32)) % N_COL
        partner = ((row_ids + row_total) % N_ROW * N_COL + (col_ids + col_total) % N_COL).astype(jnp.int32)
        tiles = pair_counts[turn].reshape(blocks, SRC_DEV, CTX_DEV)
        met = contexts[partner]
        new_src, new_met = lax.map(train_pair, (sources, met, tiles))
        sources = new_src
        contexts = contexts.at[partner].set(new_met)
    return (sources.reshape(SOURCES, D), contexts.reshape(CONTEXTS, D))
```

```python
import functools

import jax
import jax.numpy as jnp
from jax import lax
from jax.experimental import pallas as pl
from jax.experimental.pallas import tpu as pltpu
from jax.sharding import PartitionSpec as P

LEARN_RATE = 0.05
NEG_WEIGHT = 1.0
EPSILON = 1e-06
PARTS = 2
TILES = 2
NESTED_LIMIT = 32


def shifted(value, axis, by):
    length = lax.axis_size(axis)
    return lax.ppermute(value, axis, [(i, (i + by) % length) for i in range(length)])


def shifted_both(value, by_row, by_col):
    rows, cols = lax.axis_size("row"), lax.axis_size("col")
    pairs = [
        (r * cols + c, (r + by_row) % rows * cols + (c + by_col) % cols)
        for r in range(rows)
        for c in range(cols)
    ]
    return lax.ppermute(value, ("row", "col"), pairs)


def normalized(param, grad):
    scale = lax.rsqrt(jnp.mean(grad * grad, axis=1, keepdims=True) + EPSILON)
    return param - LEARN_RATE * grad * scale


def tiles_of(rows, body):
    tile = rows // TILES
    if TILES == 1:
        body(pl.ds(0, rows))
        return

    def step(index, carry):
        body(pl.ds(pl.multiple_of(index * tile, tile), tile))
        return carry

    lax.fori_loop(0, TILES, step, 0)


def couple(src_low, ctx_low, weight_ref, here, grad_ctx_ref):
    scores = lax.dot_general(
        src_low, ctx_low, (((1,), (1,)), ((), ())), preferred_element_type=jnp.float32
    )
    weight = weight_ref[here, :].astype(jnp.float32)
    coef = ((weight + NEG_WEIGHT) * jax.nn.sigmoid(scores) - weight).astype(jnp.bfloat16)
    grad_ctx = lax.dot_general(
        coef, src_low, (((0,), (0,)), ((), ())), preferred_element_type=jnp.float32
    )
    if TILES == 1:
        grad_ctx_ref[...] = grad_ctx
    else:
        grad_ctx_ref[...] += grad_ctx
    return coef


def fetch_counts(counts_ref, turn, part, size, weight_ref, arrived):
    copy = pltpu.make_async_copy(
        counts_ref.at[turn, :, pl.ds(part * size, size)], weight_ref, arrived
    )
    copy.start()
    return copy


def early_part(src_ref, ctx_ref, weight_ref, copy, new_ctx_ref, coef_ref, low_ref, grad_ctx_ref):
    low_ref[...] = ctx_ref[...].astype(jnp.bfloat16)
    if TILES > 1:
        grad_ctx_ref[...] = jnp.zeros_like(grad_ctx_ref)
    copy.wait()

    def body(here):
        src_low = src_ref[here, :].astype(jnp.bfloat16)
        coef_ref[here, :] = couple(src_low, low_ref[...], weight_ref, here, grad_ctx_ref)

    tiles_of(src_ref.shape[0], body)
    new_ctx_ref[...] = normalized(ctx_ref[...], grad_ctx_ref[...])


def last_part(src_ref, ctx_ref, weight_ref, copy, earlier, new_src_ref, src_low_ref, new_ctx_ref, low_ref, grad_ctx_ref):
    low_ref[...] = ctx_ref[...].astype(jnp.bfloat16)
    if TILES > 1:
        grad_ctx_ref[...] = jnp.zeros_like(grad_ctx_ref)
    copy.wait()

    def body(here):
        src = src_ref[here, :]
        ctx_low = low_ref[...]
        coef = couple(src.astype(jnp.bfloat16), ctx_low, weight_ref, here, grad_ctx_ref)
        grad_src = jnp.dot(coef, ctx_low, preferred_element_type=jnp.float32)
        if earlier:
            coef_ref, early_ref = earlier
            grad_src = grad_src + jnp.dot(
                coef_ref[here, :], early_ref[...], preferred_element_type=jnp.float32
            )
        new_src = normalized(src, grad_src)
        new_src_ref[here, :] = new_src
        if src_low_ref is not None:
            src_low_ref[here, :] = new_src.astype(jnp.bfloat16)

    tiles_of(src_ref.shape[0], body)
    new_ctx_ref[...] = normalized(ctx_ref[...], grad_ctx_ref[...])


def launch(body, operands, counts, out_shape, scratch_shapes, rows, size, width, pieces):
    whole = pl.BlockSpec(memory_space=pltpu.VMEM)
    return pl.pallas_call(
        body,
        in_specs=[whole] * len(operands) + [pl.BlockSpec(memory_space=pltpu.HBM)],
        out_specs=[whole] * len(out_shape),
        out_shape=out_shape,
        scratch_shapes=scratch_shapes,
        compiler_params=pltpu.CompilerParams(vmem_limit_bytes=16 * 1024 * 1024),
        cost_estimate=pl.CostEstimate(
            flops=6 * rows * size * width * pieces,
            bytes_accessed=4 * (2 * rows * width + pieces * (2 * size * width + rows * size)),
            transcendentals=rows * size * pieces,
        ),
    )(*operands, counts)


def shapes_for(rows, size, width):
    src = jax.ShapeDtypeStruct((rows, width), jnp.float32)
    src_low = jax.ShapeDtypeStruct((rows, width), jnp.bfloat16)
    ctx = jax.ShapeDtypeStruct((size, width), jnp.float32)
    coef = jax.ShapeDtypeStruct((rows, size), jnp.bfloat16)
    low = jax.ShapeDtypeStruct((size, width), jnp.bfloat16)
    return src, src_low, ctx, coef, low


def train_early(turn, src, ctx, counts):
    (rows, width), size = src.shape, ctx.shape[0]
    _, _, ctx_t, coef_t, low_t = shapes_for(rows, size, width)

    def body(src_ref, ctx_ref, counts_ref, new_ctx_ref, coef_ref, low_ref, weight_ref, grad_ref, arrived):
        copy = fetch_counts(counts_ref, turn, 0, size, weight_ref, arrived)
        early_part(src_ref, ctx_ref, weight_ref, copy, new_ctx_ref, coef_ref, low_ref, grad_ref)

    scratch = [pltpu.VMEM((rows, size), jnp.int32), pltpu.VMEM((size, width), jnp.float32), pltpu.SemaphoreType.DMA]
    return launch(body, [src, ctx], counts, [ctx_t, coef_t, low_t], scratch, rows, size, width, 1)


def train_last(turn, part, src, ctx, earlier, counts, want_low):
    (rows, width), size = src.shape, ctx.shape[0]
    src_t, src_low_t, ctx_t, _, _ = shapes_for(rows, size, width)

    def body(src_ref, ctx_ref, *refs):
        refs = list(refs)
        early_refs = [refs.pop(0) for _ in earlier]
        counts_ref, new_src_ref = refs.pop(0), refs.pop(0)
        src_low_ref = refs.pop(0) if want_low else None
        new_ctx_ref, weight_ref, low_ref, grad_ref, arrived = refs
        copy = fetch_counts(counts_ref, turn, part, size, weight_ref, arrived)
        last_part(src_ref, ctx_ref, weight_ref, copy, early_refs, new_src_ref, src_low_ref, new_ctx_ref, low_ref, grad_ref)

    scratch = [
        pltpu.VMEM((rows, size), jnp.int32),
        pltpu.VMEM((size, width), jnp.bfloat16),
        pltpu.VMEM((size, width), jnp.float32),
        pltpu.SemaphoreType.DMA,
    ]
    outs = [src_t] + ([src_low_t] if want_low else []) + [ctx_t]
    return launch(body, [src, ctx, *earlier], counts, outs, scratch, rows, size, width, 1)


def train_seam(turn, src, ctx_b, earlier, ctx_a, counts):
    (rows, width), size = src.shape, ctx_a.shape[0]
    src_t, src_low_t, ctx_t, coef_t, low_t = shapes_for(rows, size, width)

    def body(src_ref, b_ref, coef_in, low_in, a_ref, counts_ref, new_src_ref, new_b_ref, new_a_ref, coef_ref, low_ref,
             weight_b, weight_a, src_low_ref, low_b, grad_ref, arrived):
        copy_b = fetch_counts(counts_ref, turn, 1, size, weight_b, arrived.at[0])
        copy_a = fetch_counts(counts_ref, turn + 1, 0, size, weight_a, arrived.at[1])
        last_part(src_ref, b_ref, weight_b, copy_b, [coef_in, low_in], new_src_ref, src_low_ref, new_b_ref, low_b, grad_ref)
        early_part(src_low_ref, a_ref, weight_a, copy_a, new_a_ref, coef_ref, low_ref, grad_ref)

    scratch = [
        pltpu.VMEM((rows, size), jnp.int32),
        pltpu.VMEM((rows, size), jnp.int32),
        pltpu.VMEM((rows, width), jnp.bfloat16),
        pltpu.VMEM((size, width), jnp.bfloat16),
        pltpu.VMEM((size, width), jnp.float32),
        pltpu.SemaphoreType.DMA((2,)),
    ]
    outs = [src_t, ctx_t, ctx_t, coef_t, low_t]
    return launch(body, [src, ctx_b, *earlier, ctx_a], counts, outs, scratch, rows, size, width, 2)


def col_move(block, offset, back=False, may_stay=False):
    count = lax.axis_size("col")
    branches = [
        functools.partial(shifted, axis="col", by=step if back else count - step)
        for step in range(1, count)
    ]
    if may_stay:
        return lax.switch(offset, [lambda value: value] + branches, block)
    return lax.switch(offset - 1, branches, block)


def row_move(block, offset, back=False, may_stay=False):
    count = lax.axis_size("row")
    branches = [
        functools.partial(shifted, axis="row", by=step if back else count - step)
        for step in range(1, count)
    ]
    if may_stay:
        return lax.switch(offset, [lambda value: value] + branches, block)
    return lax.switch(offset - 1, branches, block)


def totals(partner_masks, rounds):
    row_count = lax.axis_size("row")
    col_count = lax.axis_size("col")
    row_total, col_total = partner_masks[0], partner_masks[1]
    for turn in range(2, rounds, 2):
        row_total = row_total + partner_masks[turn]
        row_total = jnp.where(row_total >= row_count, row_total - row_count, row_total)
        col_total = col_total + partner_masks[turn + 1]
        col_total = jnp.where(col_total >= col_count, col_total - col_count, col_total)
    return row_total, col_total


def per_device_plain(source, context, pair_counts, partner_masks):
    rounds = pair_counts.shape[0]
    for turn in range(rounds):
        move = row_move if turn % 2 == 0 else col_move
        context = move(context, partner_masks[turn])
        source, context = train_last(turn, 0, source, context, [], pair_counts, False)
    row_total, col_total = totals(partner_masks, rounds)
    context = row_move(context, row_total, back=True, may_stay=True)
    return source, col_move(context, col_total, back=True, may_stay=True)


def per_device(source, context, pair_counts, partner_masks):
    rounds = pair_counts.shape[0]
    row_count = lax.axis_size("row")
    col_count = lax.axis_size("col")
    size = context.shape[0] // PARTS
    part_a, part_b = context[:size], context[size:]

    def opening(by, src, part_a, part_b, masks):
        part_a = shifted(part_a, "row", by)
        part_b = shifted(part_b, "row", by)
        part_a, *early = train_early(0, src, part_a, pair_counts)
        part_a = col_move(part_a, masks[1])
        return early, part_a, part_b

    def middle(turn, by, src, early, part_a, part_b, masks):
        part_a = shifted(part_a, "row", by)
        part_b = col_move(part_b, masks[turn - 1])
        src, src_low, part_b = train_last(turn - 1, 1, src, part_b, early, pair_counts, True)
        part_b = shifted(part_b, "row", by)
        part_a, *early = train_early(turn, src_low, part_a, pair_counts)
        part_a = col_move(part_a, masks[turn + 1])
        return src, early, part_a, part_b

    early, part_a, part_b = lax.switch(
        partner_masks[0] - 1,
        [functools.partial(opening, row_count - step) for step in range(1, row_count)],
        source, part_a, part_b, partner_masks,
    )
    masks, part_a = lax.optimization_barrier((partner_masks, part_a))
    src, part_b, part_a, *early = train_seam(0, source, part_b, early, part_a, pair_counts)
    for turn in range(2, rounds, 2):
        src, early, part_a, part_b = lax.switch(
            masks[turn] - 1,
            [functools.partial(middle, turn, row_count - step) for step in range(1, row_count)],
            src, early, part_a, part_b, masks,
        )
        src, part_b, part_a, *early = train_seam(turn, src, part_b, early, part_a, pair_counts)
    row_total, col_total = totals(masks, rounds)

    def returning(by_col, part_a, part_b):
        part_b = shifted(part_b, "col", by_col)
        return row_move(part_a, row_total, back=True, may_stay=True), part_b

    part_a, part_b = lax.switch(
        masks[rounds - 1] - 1,
        [functools.partial(returning, col_count - step) for step in range(1, col_count)],
        part_a, part_b,
    )
    src, part_b = train_last(rounds - 1, 1, src, part_b, early, pair_counts, False)

    def closing(by_col, part_a, part_b):
        part_a = shifted(part_a, "col", by_col) if by_col else part_a
        homeward = [
            functools.partial(shifted_both, by_row=by_row, by_col=by_col)
            if by_row or by_col
            else (lambda value: value)
            for by_row in range(row_count)
        ]
        return part_a, lax.switch(row_total, homeward, part_b)

    part_a, part_b = lax.switch(
        col_total, [functools.partial(closing, step) for step in range(col_count)], part_a, part_b
    )
    return src, jnp.concatenate([part_a, part_b], axis=0)


def solution(mesh):
    in_specs = (
        P(("row", "col"), None),
        P(("row", "col"), None),
        P(None, ("row", "col"), None),
        P(),
    )
    out_specs = (P(("row", "col"), None), P(("row", "col"), None))
    few = mesh.shape["row"] * mesh.shape["col"] <= NESTED_LIMIT
    return jax.shard_map(
        per_device if few else per_device_plain, mesh=mesh, in_specs=in_specs, out_specs=out_specs, check_vma=False
    )
```

```python
import functools

import jax
import jax.numpy as jnp
from jax import lax
from jax.experimental import pallas as pl
from jax.experimental.pallas import tpu as pltpu
from jax.sharding import PartitionSpec as P

LEARN_RATE = 0.05
NEG_WEIGHT = 1.0
EPSILON = 1e-06
PARTS = 2
INNER_TILES = 2
OUTER_TILES = 1
NESTED_LIMIT = 32


def shifted(value, axis, by):
    length = lax.axis_size(axis)
    return lax.ppermute(value, axis, [(i, (i + by) % length) for i in range(length)])


def shifted_both(value, by_row, by_col):
    rows, cols = lax.axis_size("row"), lax.axis_size("col")
    pairs = [
        (r * cols + c, (r + by_row) % rows * cols + (c + by_col) % cols)
        for r in range(rows)
        for c in range(cols)
    ]
    return lax.ppermute(value, ("row", "col"), pairs)


def normalized(param, grad):
    scale = lax.rsqrt(jnp.mean(grad * grad, axis=1, keepdims=True) + EPSILON)
    return param - LEARN_RATE * grad * scale


def tiles_of(rows, tiles, body):
    tile = rows // tiles
    if tiles == 1:
        body(pl.ds(0, rows))
        return

    def step(index, carry):
        body(pl.ds(pl.multiple_of(index * tile, tile), tile))
        return carry

    lax.fori_loop(0, tiles, step, 0)


def couple(tiles, src_low, ctx_low, weight_ref, here, grad_ctx_ref):
    scores = lax.dot_general(
        src_low, ctx_low, (((1,), (1,)), ((), ())), preferred_element_type=jnp.float32
    )
    weight = weight_ref[here, :].astype(jnp.float32)
    coef = ((weight + NEG_WEIGHT) * jax.nn.sigmoid(scores) - weight).astype(jnp.bfloat16)
    grad_ctx = lax.dot_general(
        coef, src_low, (((0,), (0,)), ((), ())), preferred_element_type=jnp.float32
    )
    if tiles == 1:
        grad_ctx_ref[...] = grad_ctx
    else:
        grad_ctx_ref[...] += grad_ctx
    return coef


def early_part(tiles, src_ref, ctx_ref, weight_ref, new_ctx_ref, coef_ref, low_ref, grad_ctx_ref):
    low_ref[...] = ctx_ref[...].astype(jnp.bfloat16)
    if tiles > 1:
        grad_ctx_ref[...] = jnp.zeros_like(grad_ctx_ref)

    def body(here):
        coef_ref[here, :] = couple(tiles, src_ref[here, :], low_ref[...], weight_ref, here, grad_ctx_ref)

    tiles_of(src_ref.shape[0], tiles, body)
    new_ctx_ref[...] = normalized(ctx_ref[...], grad_ctx_ref[...])


def last_part(tiles, src_ref, ctx_ref, weight_ref, earlier, new_src_ref, src_low_ref, new_ctx_ref, low_ref, grad_ctx_ref):
    low_ref[...] = ctx_ref[...].astype(jnp.bfloat16)
    if tiles > 1:
        grad_ctx_ref[...] = jnp.zeros_like(grad_ctx_ref)

    def body(here):
        src = src_ref[here, :]
        ctx_low = low_ref[...]
        coef = couple(tiles, src.astype(jnp.bfloat16), ctx_low, weight_ref, here, grad_ctx_ref)
        grad_src = jnp.dot(coef, ctx_low, preferred_element_type=jnp.float32)
        if earlier:
            coef_ref, early_ref = earlier
            grad_src = grad_src + jnp.dot(
                coef_ref[here, :], early_ref[...], preferred_element_type=jnp.float32
            )
        new_src = normalized(src, grad_src)
        new_src_ref[here, :] = new_src
        if src_low_ref is not None:
            src_low_ref[here, :] = new_src.astype(jnp.bfloat16)

    tiles_of(src_ref.shape[0], tiles, body)
    new_ctx_ref[...] = normalized(ctx_ref[...], grad_ctx_ref[...])


def launch(body, operands, out_shape, scratch_shapes, rows, size, width, pieces):
    whole = pl.BlockSpec(memory_space=pltpu.VMEM)
    return pl.pallas_call(
        body,
        in_specs=[whole] * len(operands),
        out_specs=[whole] * len(out_shape),
        out_shape=out_shape,
        scratch_shapes=scratch_shapes,
        compiler_params=pltpu.CompilerParams(vmem_limit_bytes=12 * 1024 * 1024),
        cost_estimate=pl.CostEstimate(
            flops=6 * rows * size * width * pieces,
            bytes_accessed=4 * (2 * rows * width + pieces * (2 * size * width + rows * size)),
            transcendentals=rows * size * pieces,
        ),
    )(*operands)


def shapes_for(rows, size, width):
    src = jax.ShapeDtypeStruct((rows, width), jnp.float32)
    src_low = jax.ShapeDtypeStruct((rows, width), jnp.bfloat16)
    ctx = jax.ShapeDtypeStruct((size, width), jnp.float32)
    coef = jax.ShapeDtypeStruct((rows, size), jnp.bfloat16)
    low = jax.ShapeDtypeStruct((size, width), jnp.bfloat16)
    return src, src_low, ctx, coef, low


def stage(source, counts, parts):
    (rows, width), rounds = source.shape, counts.shape[0]
    size = counts.shape[2] // parts
    tile = min(64, rows)

    def body(src_ref, counts_ref, copy_ref, low_ref, *weight_refs):
        copy_ref[...] = src_ref[...]
        low_ref[...] = src_ref[...].astype(jnp.bfloat16)
        for index, weight_ref in enumerate(weight_refs):
            turn, part = divmod(index, parts)
            weight_ref[...] = (
                counts_ref[turn, :, part * size : (part + 1) * size]
                .astype(jnp.float32)
                .astype(jnp.bfloat16)
            )

    src_spec = pl.BlockSpec((tile, width), lambda i: (i, 0))
    weight_spec = pl.BlockSpec((tile, size), lambda i: (i, 0))
    src_t, src_low_t, _, weight_t, _ = shapes_for(rows, size, width)
    return pl.pallas_call(
        body,
        grid=(rows // tile,),
        in_specs=[src_spec, pl.BlockSpec((rounds, tile, parts * size), lambda i: (0, i, 0))],
        out_specs=[src_spec, src_spec] + [weight_spec] * (rounds * parts),
        out_shape=[src_t, src_low_t] + [weight_t] * (rounds * parts),
        compiler_params=pltpu.CompilerParams(
            dimension_semantics=("arbitrary",), vmem_limit_bytes=8 * 1024 * 1024
        ),
        cost_estimate=pl.CostEstimate(
            flops=rounds * rows * size * parts,
            bytes_accessed=6 * rounds * rows * size * parts + 10 * rows * width,
            transcendentals=0,
        ),
    )(source, counts)


def train_early(src_low, ctx, weight):
    (rows, width), size = src_low.shape, ctx.shape[0]
    _, _, ctx_t, coef_t, low_t = shapes_for(rows, size, width)

    def body(*refs):
        early_part(INNER_TILES, *refs)

    scratch = [pltpu.VMEM((size, width), jnp.float32)]
    return launch(body, [src_low, ctx, weight], [ctx_t, coef_t, low_t], scratch, rows, size, width, 1)


def train_last(tiles, src, ctx, weight, earlier, want_low):
    (rows, width), size = src.shape, ctx.shape[0]
    src_t, src_low_t, ctx_t, _, _ = shapes_for(rows, size, width)

    def body(src_ref, ctx_ref, weight_ref, *refs):
        refs = list(refs)
        early_refs = [refs.pop(0) for _ in earlier]
        new_src_ref = refs.pop(0)
        src_low_ref = refs.pop(0) if want_low else None
        last_part(tiles, src_ref, ctx_ref, weight_ref, early_refs, new_src_ref, src_low_ref, *refs)

    scratch = [pltpu.VMEM((size, width), jnp.bfloat16), pltpu.VMEM((size, width), jnp.float32)]
    outs = [src_t] + ([src_low_t] if want_low else []) + [ctx_t]
    return launch(body, [src, ctx, weight, *earlier], outs, scratch, rows, size, width, 1)


def train_seam(src, ctx_b, weight_b, earlier, ctx_a, weight_a):
    (rows, width), size = src.shape, ctx_a.shape[0]
    src_t, src_low_t, ctx_t, coef_t, low_t = shapes_for(rows, size, width)

    def body(src_ref, b_ref, weight_b_ref, coef_in, low_in, a_ref, weight_a_ref,
             new_src_ref, new_b_ref, new_a_ref, coef_ref, low_ref, src_low_ref, low_b_ref, grad_ref):
        last_part(OUTER_TILES, src_ref, b_ref, weight_b_ref, [coef_in, low_in], new_src_ref, src_low_ref, new_b_ref, low_b_ref, grad_ref)
        early_part(OUTER_TILES, src_low_ref, a_ref, weight_a_ref, new_a_ref, coef_ref, low_ref, grad_ref)

    scratch = [
        pltpu.VMEM((rows, width), jnp.bfloat16),
        pltpu.VMEM((size, width), jnp.bfloat16),
        pltpu.VMEM((size, width), jnp.float32),
    ]
    outs = [src_t, ctx_t, ctx_t, coef_t, low_t]
    return launch(body, [src, ctx_b, weight_b, *earlier, ctx_a, weight_a], outs, scratch, rows, size, width, 2)


def col_move(block, offset, back=False, may_stay=False):
    count = lax.axis_size("col")
    branches = [
        functools.partial(shifted, axis="col", by=step if back else count - step)
        for step in range(1, count)
    ]
    if may_stay:
        return lax.switch(offset, [lambda value: value] + branches, block)
    return lax.switch(offset - 1, branches, block)


def row_move(block, offset, back=False, may_stay=False):
    count = lax.axis_size("row")
    branches = [
        functools.partial(shifted, axis="row", by=step if back else count - step)
        for step in range(1, count)
    ]
    if may_stay:
        return lax.switch(offset, [lambda value: value] + branches, block)
    return lax.switch(offset - 1, branches, block)


def totals(partner_masks, rounds):
    row_count = lax.axis_size("row")
    col_count = lax.axis_size("col")
    row_total, col_total = partner_masks[0], partner_masks[1]
    for turn in range(2, rounds, 2):
        row_total = row_total + partner_masks[turn]
        row_total = jnp.where(row_total >= row_count, row_total - row_count, row_total)
        col_total = col_total + partner_masks[turn + 1]
        col_total = jnp.where(col_total >= col_count, col_total - col_count, col_total)
    return row_total, col_total


def per_device_plain(source, context, pair_counts, partner_masks):
    rounds = pair_counts.shape[0]
    for turn in range(rounds):
        move = row_move if turn % 2 == 0 else col_move
        context = move(context, partner_masks[turn])
        source, context = train_last(OUTER_TILES, source, context, pair_counts[turn], [], False)
    row_total, col_total = totals(partner_masks, rounds)
    context = row_move(context, row_total, back=True, may_stay=True)
    return source, col_move(context, col_total, back=True, may_stay=True)


def per_device(source, context, pair_counts, partner_masks):
    rounds = pair_counts.shape[0]
    row_count = lax.axis_size("row")
    col_count = lax.axis_size("col")
    size = context.shape[0] // PARTS
    part_a, part_b = context[:size], context[size:]

    def opening(by, src, counts, part_a, part_b, masks):
        part_a = shifted(part_a, "row", by)
        part_b = shifted(part_b, "row", by)
        src, src_low, *weights = stage(src, counts, PARTS)
        part_a, *early = train_early(src_low, part_a, weights[0])
        part_a = col_move(part_a, masks[1])
        return src, weights[1:], early, part_a, part_b, totals(masks, rounds)

    def middle(turn, by, src, early, part_a, part_b, weights, masks):
        part_a = shifted(part_a, "row", by)
        part_b = col_move(part_b, masks[turn - 1])
        src, src_low, part_b = train_last(INNER_TILES, src, part_b, weights[0], early, True)
        part_b = shifted(part_b, "row", by)
        part_a, *early = train_early(src_low, part_a, weights[1])
        part_a = col_move(part_a, masks[turn + 1])
        return src, early, part_a, part_b

    src, weights, early, part_a, part_b, (row_total, col_total) = lax.switch(
        partner_masks[0] - 1,
        [functools.partial(opening, row_count - step) for step in range(1, row_count)],
        source, pair_counts, part_a, part_b, partner_masks,
    )
    weights = [None] + list(weights)
    src, part_b, part_a, *early = train_seam(src, part_b, weights[1], early, part_a, weights[2])
    for turn in range(2, rounds, 2):
        here = PARTS * turn
        src, early, part_a, part_b = lax.switch(
            partner_masks[turn] - 1,
            [functools.partial(middle, turn, row_count - step) for step in range(1, row_count)],
            src, early, part_a, part_b, weights[here - 1 : here + 1], partner_masks,
        )
        src, part_b, part_a, *early = train_seam(
            src, part_b, weights[here + 1], early, part_a, weights[here + 2]
        )

    def returning(by_row, part_a, part_b):
        part_a = shifted(part_a, "row", by_row) if by_row else part_a
        return part_a, col_move(part_b, partner_masks[rounds - 1])

    part_a, part_b = lax.switch(
        row_total, [functools.partial(returning, step) for step in range(row_count)], part_a, part_b
    )
    src, part_b = train_last(OUTER_TILES, src, part_b, weights[-1], early, False)

    def closing(by_col, part_a, part_b):
        part_a = shifted(part_a, "col", by_col) if by_col else part_a
        homeward = [
            functools.partial(shifted_both, by_row=by_row, by_col=by_col)
            if by_row or by_col
            else (lambda value: value)
            for by_row in range(row_count)
        ]
        return part_a, lax.switch(row_total, homeward, part_b)

    part_a, part_b = lax.switch(
        col_total, [functools.partial(closing, step) for step in range(col_count)], part_a, part_b
    )
    return src, jnp.concatenate([part_a, part_b], axis=0)


def solution(mesh):
    in_specs = (
        P(("row", "col"), None),
        P(("row", "col"), None),
        P(None, ("row", "col"), None),
        P(),
    )
    out_specs = (P(("row", "col"), None), P(("row", "col"), None))
    few = mesh.shape["row"] * mesh.shape["col"] <= NESTED_LIMIT
    return jax.shard_map(
        per_device if few else per_device_plain, mesh=mesh, in_specs=in_specs, out_specs=out_specs, check_vma=False
    )
```

```python
import functools

import jax
import jax.numpy as jnp
from jax import lax
from jax.experimental import pallas as pl
from jax.experimental.pallas import tpu as pltpu
from jax.sharding import PartitionSpec as P

LEARN_RATE = 0.05
NEG_WEIGHT = 1.0
EPSILON = 1e-06
PARTS = 2
INNER_TILES = 2
OUTER_TILES = 1
CTX_TILES = 2
NESTED_LIMIT = 32


def shifted(value, axis, by):
    length = lax.axis_size(axis)
    return lax.ppermute(value, axis, [(i, (i + by) % length) for i in range(length)])


def shifted_both(value, by_row, by_col):
    rows, cols = lax.axis_size("row"), lax.axis_size("col")
    pairs = [
        (r * cols + c, (r + by_row) % rows * cols + (c + by_col) % cols)
        for r in range(rows)
        for c in range(cols)
    ]
    return lax.ppermute(value, ("row", "col"), pairs)


def normalized(param, grad):
    scale = lax.rsqrt(jnp.mean(grad * grad, axis=1, keepdims=True) + EPSILON)
    return param - LEARN_RATE * grad * scale


def tiles_of(rows, tiles, body):
    tile = rows // tiles
    if tiles == 1:
        body(pl.ds(0, rows))
        return

    def step(index, carry):
        body(pl.ds(pl.multiple_of(index * tile, tile), tile))
        return carry

    lax.fori_loop(0, tiles, step, 0)


def couple(tiles, src_low, ctx_low, weight_ref, here, grad_ctx_ref):
    scores = lax.dot_general(
        src_low, ctx_low, (((1,), (1,)), ((), ())), preferred_element_type=jnp.float32
    )
    weight = weight_ref[here, :].astype(jnp.float32)
    coef = ((weight + NEG_WEIGHT) * jax.nn.sigmoid(scores) - weight).astype(jnp.bfloat16)
    grad_ctx = lax.dot_general(
        coef, src_low, (((0,), (0,)), ((), ())), preferred_element_type=jnp.float32
    )
    if tiles == 1:
        grad_ctx_ref[...] = grad_ctx
    else:
        grad_ctx_ref[...] += grad_ctx
    return coef


def round_ctx(tiles, ctx_ref, low_ref, grad_ctx_ref):
    def body(here):
        ctx = ctx_ref[here, :]
        low_ref[here, :] = ctx.astype(jnp.bfloat16)
        if tiles > 1:
            grad_ctx_ref[here, :] = jnp.zeros_like(ctx)

    tiles_of(ctx_ref.shape[0], CTX_TILES if tiles > 1 else 1, body)


def update_ctx(tiles, ctx_ref, grad_ctx_ref, new_ctx_ref):
    def body(here):
        new_ctx_ref[here, :] = normalized(ctx_ref[here, :], grad_ctx_ref[here, :])

    tiles_of(ctx_ref.shape[0], CTX_TILES if tiles > 1 else 1, body)


def early_part(tiles, src_ref, ctx_ref, weight_ref, new_ctx_ref, coef_ref, low_ref, grad_ctx_ref):
    round_ctx(tiles, ctx_ref, low_ref, grad_ctx_ref)

    def body(here):
        coef_ref[here, :] = couple(tiles, src_ref[here, :], low_ref[...], weight_ref, here, grad_ctx_ref)

    tiles_of(src_ref.shape[0], tiles, body)
    update_ctx(tiles, ctx_ref, grad_ctx_ref, new_ctx_ref)


def last_part(tiles, src_ref, ctx_ref, weight_ref, earlier, new_src_ref, src_low_ref, new_ctx_ref, low_ref, grad_ctx_ref):
    round_ctx(tiles, ctx_ref, low_ref, grad_ctx_ref)

    def body(here):
        src = src_ref[here, :]
        ctx_low = low_ref[...]
        coef = couple(tiles, src.astype(jnp.bfloat16), ctx_low, weight_ref, here, grad_ctx_ref)
        grad_src = jnp.dot(coef, ctx_low, preferred_element_type=jnp.float32)
        if earlier:
            coef_ref, early_ref = earlier
            grad_src = grad_src + jnp.dot(
                coef_ref[here, :], early_ref[...], preferred_element_type=jnp.float32
            )
        new_src = normalized(src, grad_src)
        new_src_ref[here, :] = new_src
        if src_low_ref is not None:
            src_low_ref[here, :] = new_src.astype(jnp.bfloat16)

    tiles_of(src_ref.shape[0], tiles, body)
    update_ctx(tiles, ctx_ref, grad_ctx_ref, new_ctx_ref)


def launch(body, operands, out_shape, scratch_shapes, rows, size, width, pieces):
    whole = pl.BlockSpec(memory_space=pltpu.VMEM)
    return pl.pallas_call(
        body,
        in_specs=[whole] * len(operands),
        out_specs=[whole] * len(out_shape),
        out_shape=out_shape,
        scratch_shapes=scratch_shapes,
        compiler_params=pltpu.CompilerParams(vmem_limit_bytes=12 * 1024 * 1024),
        cost_estimate=pl.CostEstimate(
            flops=6 * rows * size * width * pieces,
            bytes_accessed=4 * (2 * rows * width + pieces * (2 * size * width + rows * size)),
            transcendentals=rows * size * pieces,
        ),
    )(*operands)


def shapes_for(rows, size, width):
    src = jax.ShapeDtypeStruct((rows, width), jnp.float32)
    src_low = jax.ShapeDtypeStruct((rows, width), jnp.bfloat16)
    ctx = jax.ShapeDtypeStruct((size, width), jnp.float32)
    coef = jax.ShapeDtypeStruct((rows, size), jnp.bfloat16)
    low = jax.ShapeDtypeStruct((size, width), jnp.bfloat16)
    return src, src_low, ctx, coef, low


def stage(source, counts, parts):
    (rows, width), rounds = source.shape, counts.shape[0]
    size = counts.shape[2] // parts
    tile = min(128, rows)

    def body(src_ref, counts_ref, copy_ref, low_ref, *weight_refs):
        copy_ref[...] = src_ref[...]
        low_ref[...] = src_ref[...].astype(jnp.bfloat16)
        for index, weight_ref in enumerate(weight_refs):
            turn, part = divmod(index, parts)
            weight_ref[...] = (
                counts_ref[turn, :, part * size : (part + 1) * size]
                .astype(jnp.float32)
                .astype(jnp.bfloat16)
            )

    src_spec = pl.BlockSpec((tile, width), lambda i: (i, 0))
    weight_spec = pl.BlockSpec((tile, size), lambda i: (i, 0))
    src_t, src_low_t, _, weight_t, _ = shapes_for(rows, size, width)
    return pl.pallas_call(
        body,
        grid=(rows // tile,),
        in_specs=[src_spec, pl.BlockSpec((rounds, tile, parts * size), lambda i: (0, i, 0))],
        out_specs=[src_spec, src_spec] + [weight_spec] * (rounds * parts),
        out_shape=[src_t, src_low_t] + [weight_t] * (rounds * parts),
        compiler_params=pltpu.CompilerParams(
            dimension_semantics=("arbitrary",), vmem_limit_bytes=8 * 1024 * 1024
        ),
        cost_estimate=pl.CostEstimate(
            flops=rounds * rows * size * parts,
            bytes_accessed=6 * rounds * rows * size * parts + 10 * rows * width,
            transcendentals=0,
        ),
    )(source, counts)


def join(part_a, part_b):
    size, width = part_a.shape

    def body(a_ref, b_ref, out_ref, arrived):
        copies = [
            pltpu.make_async_copy(a_ref, out_ref.at[pl.ds(0, size)], arrived.at[0]),
            pltpu.make_async_copy(b_ref, out_ref.at[pl.ds(size, size)], arrived.at[1]),
        ]
        for copy in copies:
            copy.start()
        for copy in copies:
            copy.wait()

    return pl.pallas_call(
        body,
        in_specs=[pl.BlockSpec(memory_space=pltpu.VMEM)] * 2,
        out_specs=pl.BlockSpec(memory_space=pltpu.HBM),
        out_shape=jax.ShapeDtypeStruct((2 * size, width), jnp.float32),
        scratch_shapes=[pltpu.SemaphoreType.DMA((2,))],
        compiler_params=pltpu.CompilerParams(vmem_limit_bytes=4 * 1024 * 1024),
    )(part_a, part_b)


def train_early(src_low, ctx, weight):
    (rows, width), size = src_low.shape, ctx.shape[0]
    _, _, ctx_t, coef_t, low_t = shapes_for(rows, size, width)

    def body(*refs):
        early_part(INNER_TILES, *refs)

    scratch = [pltpu.VMEM((size, width), jnp.float32)]
    return launch(body, [src_low, ctx, weight], [ctx_t, coef_t, low_t], scratch, rows, size, width, 1)


def train_last(tiles, src, ctx, weight, earlier, want_low):
    (rows, width), size = src.shape, ctx.shape[0]
    src_t, src_low_t, ctx_t, _, _ = shapes_for(rows, size, width)

    def body(src_ref, ctx_ref, weight_ref, *refs):
        refs = list(refs)
        early_refs = [refs.pop(0) for _ in earlier]
        new_src_ref = refs.pop(0)
        src_low_ref = refs.pop(0) if want_low else None
        last_part(tiles, src_ref, ctx_ref, weight_ref, early_refs, new_src_ref, src_low_ref, *refs)

    scratch = [pltpu.VMEM((size, width), jnp.bfloat16), pltpu.VMEM((size, width), jnp.float32)]
    outs = [src_t] + ([src_low_t] if want_low else []) + [ctx_t]
    return launch(body, [src, ctx, weight, *earlier], outs, scratch, rows, size, width, 1)


def train_seam(src, ctx_b, weight_b, earlier, ctx_a, weight_a):
    (rows, width), size = src.shape, ctx_a.shape[0]
    src_t, src_low_t, ctx_t, coef_t, low_t = shapes_for(rows, size, width)

    def body(src_ref, b_ref, weight_b_ref, coef_in, low_in, a_ref, weight_a_ref,
             new_src_ref, new_b_ref, new_a_ref, coef_ref, low_ref, src_low_ref, low_b_ref, grad_ref):
        last_part(OUTER_TILES, src_ref, b_ref, weight_b_ref, [coef_in, low_in], new_src_ref, src_low_ref, new_b_ref, low_b_ref, grad_ref)
        early_part(OUTER_TILES, src_low_ref, a_ref, weight_a_ref, new_a_ref, coef_ref, low_ref, grad_ref)

    scratch = [
        pltpu.VMEM((rows, width), jnp.bfloat16),
        pltpu.VMEM((size, width), jnp.bfloat16),
        pltpu.VMEM((size, width), jnp.float32),
    ]
    outs = [src_t, ctx_t, ctx_t, coef_t, low_t]
    return launch(body, [src, ctx_b, weight_b, *earlier, ctx_a, weight_a], outs, scratch, rows, size, width, 2)


def col_move(block, offset, back=False, may_stay=False):
    count = lax.axis_size("col")
    branches = [
        functools.partial(shifted, axis="col", by=step if back else count - step)
        for step in range(1, count)
    ]
    if may_stay:
        return lax.switch(offset, [lambda value: value] + branches, block)
    return lax.switch(offset - 1, branches, block)


def col_hop(block, index):
    count = lax.axis_size("col")
    return lax.switch(
        index, [functools.partial(shifted, axis="col", by=count - step) for step in range(1, count)], block
    )


def row_move(block, offset, back=False, may_stay=False):
    count = lax.axis_size("row")
    branches = [
        functools.partial(shifted, axis="row", by=step if back else count - step)
        for step in range(1, count)
    ]
    if may_stay:
        return lax.switch(offset, [lambda value: value] + branches, block)
    return lax.switch(offset - 1, branches, block)


def totals(partner_masks, rounds):
    row_count = lax.axis_size("row")
    col_count = lax.axis_size("col")
    row_total, col_total = partner_masks[0], partner_masks[1]
    for turn in range(2, rounds, 2):
        row_total = row_total + partner_masks[turn]
        row_total = jnp.where(row_total >= row_count, row_total - row_count, row_total)
        col_total = col_total + partner_masks[turn + 1]
        col_total = jnp.where(col_total >= col_count, col_total - col_count, col_total)
    return row_total, col_total


def per_device_plain(source, context, pair_counts, partner_masks):
    rounds = pair_counts.shape[0]
    for turn in range(rounds):
        move = row_move if turn % 2 == 0 else col_move
        context = move(context, partner_masks[turn])
        source, context = train_last(OUTER_TILES, source, context, pair_counts[turn], [], False)
    row_total, col_total = totals(partner_masks, rounds)
    context = row_move(context, row_total, back=True, may_stay=True)
    return source, col_move(context, col_total, back=True, may_stay=True)


def per_device(source, context, pair_counts, partner_masks):
    rounds = pair_counts.shape[0]
    row_count = lax.axis_size("row")
    col_count = lax.axis_size("col")
    size = context.shape[0] // PARTS

    def opening(by, src, counts, ctx, masks):
        part_a = shifted(ctx[:size], "row", by)
        part_b = shifted(ctx[size:], "row", by)
        hops = [masks[turn] - 1 for turn in range(rounds)]
        src, src_low, *weights = stage(src, counts, PARTS)
        part_a, *early = train_early(src_low, part_a, weights[0])
        part_a = col_hop(part_a, hops[1])
        return src, weights[1:], early, part_a, part_b, totals(masks, rounds), hops

    def middle(by, src, early, part_a, part_b, weights, hop_b, hop_a):
        part_a = shifted(part_a, "row", by)
        part_b = col_hop(part_b, hop_b)
        src, src_low, part_b = train_last(INNER_TILES, src, part_b, weights[0], early, True)
        part_b = shifted(part_b, "row", by)
        part_a, *early = train_early(src_low, part_a, weights[1])
        part_a = col_hop(part_a, hop_a)
        return src, early, part_a, part_b

    src, weights, early, part_a, part_b, (row_total, col_total), hops = lax.switch(
        (partner_masks - 1)[0],
        [functools.partial(opening, row_count - step) for step in range(1, row_count)],
        source, pair_counts, context, partner_masks,
    )
    weights = [None] + list(weights)
    src, part_b, part_a, *early = train_seam(src, part_b, weights[1], early, part_a, weights[2])
    for turn in range(2, rounds, 2):
        here = PARTS * turn
        src, early, part_a, part_b = lax.switch(
            hops[turn],
            [functools.partial(middle, row_count - step) for step in range(1, row_count)],
            src, early, part_a, part_b, weights[here - 1 : here + 1], hops[turn - 1], hops[turn + 1],
        )
        src, part_b, part_a, *early = train_seam(
            src, part_b, weights[here + 1], early, part_a, weights[here + 2]
        )

    def returning(by_row, part_a, part_b):
        part_a = shifted(part_a, "row", by_row) if by_row else part_a
        return part_a, col_hop(part_b, hops[rounds - 1])

    part_a, part_b = lax.switch(
        row_total, [functools.partial(returning, step) for step in range(row_count)], part_a, part_b
    )
    src, part_b = train_last(OUTER_TILES, src, part_b, weights[-1], early, False)

    def closing(by_col, part_a, part_b):
        part_a = shifted(part_a, "col", by_col) if by_col else part_a
        homeward = [
            functools.partial(shifted_both, by_row=by_row, by_col=by_col)
            if by_row or by_col
            else (lambda value: value)
            for by_row in range(row_count)
        ]
        return part_a, lax.switch(row_total, homeward, part_b)

    part_a, part_b = lax.switch(
        col_total, [functools.partial(closing, step) for step in range(col_count)], part_a, part_b
    )
    return src, join(part_a, part_b)


def solution(mesh):
    in_specs = (
        P(("row", "col"), None),
        P(("row", "col"), None),
        P(None, ("row", "col"), None),
        P(),
    )
    out_specs = (P(("row", "col"), None), P(("row", "col"), None))
    few = mesh.shape["row"] * mesh.shape["col"] <= NESTED_LIMIT
    return jax.shard_map(
        per_device if few else per_device_plain, mesh=mesh, in_specs=in_specs, out_specs=out_specs, check_vma=False
    )
```

```python
import functools

import jax
import jax.numpy as jnp
from jax import lax
from jax.experimental import pallas as pl
from jax.experimental.pallas import tpu as pltpu
from jax.sharding import PartitionSpec as P

LEARN_RATE = 0.05
NEG_WEIGHT = 1.0
EPSILON = 1e-06
PARTS = 2
INNER_TILES = 2
OUTER_TILES = 1
CTX_TILES = 2
NESTED_LIMIT = 32


def shifted(value, axis, by):
    length = lax.axis_size(axis)
    return lax.ppermute(value, axis, [(i, (i + by) % length) for i in range(length)])


def shifted_both(value, by_row, by_col):
    rows, cols = lax.axis_size("row"), lax.axis_size("col")
    pairs = [
        (r * cols + c, (r + by_row) % rows * cols + (c + by_col) % cols)
        for r in range(rows)
        for c in range(cols)
    ]
    return lax.ppermute(value, ("row", "col"), pairs)


def normalized(param, grad):
    scale = lax.rsqrt(jnp.mean(grad * grad, axis=1, keepdims=True) + EPSILON)
    return param - LEARN_RATE * grad * scale


def tiles_of(rows, tiles, body):
    tile = rows // tiles
    if tiles == 1:
        body(pl.ds(0, rows))
        return

    def step(index, carry):
        body(pl.ds(pl.multiple_of(index * tile, tile), tile))
        return carry

    lax.fori_loop(0, tiles, step, 0)


def couple(tiles, src_low, ctx_low, weight_ref, here, grad_ctx_ref):
    scores = lax.dot_general(
        src_low, ctx_low, (((1,), (1,)), ((), ())), preferred_element_type=jnp.float32
    )
    weight = weight_ref[here, :].astype(jnp.int32).astype(jnp.float32)
    coef = ((weight + NEG_WEIGHT) * jax.nn.sigmoid(scores) - weight).astype(jnp.bfloat16)
    grad_ctx = lax.dot_general(
        coef, src_low, (((0,), (0,)), ((), ())), preferred_element_type=jnp.float32
    )
    if tiles == 1:
        grad_ctx_ref[...] = grad_ctx
    else:
        grad_ctx_ref[...] += grad_ctx
    return coef


def round_ctx(tiles, ctx_ref, low_ref, grad_ctx_ref):
    def body(here):
        ctx = ctx_ref[here, :]
        low_ref[here, :] = ctx.astype(jnp.bfloat16)
        if tiles > 1:
            grad_ctx_ref[here, :] = jnp.zeros_like(ctx)

    tiles_of(ctx_ref.shape[0], CTX_TILES if tiles > 1 else 1, body)


def update_ctx(tiles, ctx_ref, grad_ctx_ref, new_ctx_ref):
    def body(here):
        new_ctx_ref[here, :] = normalized(ctx_ref[here, :], grad_ctx_ref[here, :])

    tiles_of(ctx_ref.shape[0], CTX_TILES if tiles > 1 else 1, body)


def early_tiles(tiles, src_ref, weight_ref, coef_ref, low_ref, grad_ctx_ref):
    def body(here):
        coef_ref[here, :] = couple(tiles, src_ref[here, :], low_ref[...], weight_ref, here, grad_ctx_ref)

    tiles_of(src_ref.shape[0], tiles, body)


def early_part(tiles, src_ref, ctx_ref, weight_ref, new_ctx_ref, coef_ref, low_ref, grad_ctx_ref):
    round_ctx(tiles, ctx_ref, low_ref, grad_ctx_ref)
    early_tiles(tiles, src_ref, weight_ref, coef_ref, low_ref, grad_ctx_ref)
    update_ctx(tiles, ctx_ref, grad_ctx_ref, new_ctx_ref)


def last_part(tiles, src_ref, ctx_ref, weight_ref, earlier, new_src_ref, src_low_ref, new_ctx_ref, low_ref, grad_ctx_ref):
    round_ctx(tiles, ctx_ref, low_ref, grad_ctx_ref)

    def body(here):
        src = src_ref[here, :]
        ctx_low = low_ref[...]
        coef = couple(tiles, src.astype(jnp.bfloat16), ctx_low, weight_ref, here, grad_ctx_ref)
        grad_src = jnp.dot(coef, ctx_low, preferred_element_type=jnp.float32)
        if earlier:
            coef_ref, early_ref = earlier
            grad_src = grad_src + jnp.dot(
                coef_ref[here, :], early_ref[...], preferred_element_type=jnp.float32
            )
        new_src = normalized(src, grad_src)
        new_src_ref[here, :] = new_src
        if src_low_ref is not None:
            src_low_ref[here, :] = new_src.astype(jnp.bfloat16)

    tiles_of(src_ref.shape[0], tiles, body)
    update_ctx(tiles, ctx_ref, grad_ctx_ref, new_ctx_ref)


def launch(body, operands, out_shape, scratch_shapes, rows, size, width, pieces, kept=None):
    whole = pl.BlockSpec(memory_space=pltpu.VMEM)
    kept = len(out_shape) if kept is None else kept
    return pl.pallas_call(
        body,
        in_specs=[whole] * len(operands),
        out_specs=[whole] * kept + [pl.BlockSpec(memory_space=pl.ANY)] * (len(out_shape) - kept),
        out_shape=out_shape,
        scratch_shapes=scratch_shapes,
        compiler_params=pltpu.CompilerParams(vmem_limit_bytes=12 * 1024 * 1024),
        cost_estimate=pl.CostEstimate(
            flops=6 * rows * size * width * pieces,
            bytes_accessed=4 * (2 * rows * width + pieces * (2 * size * width + rows * size)),
            transcendentals=rows * size * pieces,
        ),
    )(*operands)


def shapes_for(rows, size, width):
    src = jax.ShapeDtypeStruct((rows, width), jnp.float32)
    src_low = jax.ShapeDtypeStruct((rows, width), jnp.bfloat16)
    ctx = jax.ShapeDtypeStruct((size, width), jnp.float32)
    coef = jax.ShapeDtypeStruct((rows, size), jnp.bfloat16)
    low = jax.ShapeDtypeStruct((size, width), jnp.bfloat16)
    return src, src_low, ctx, coef, low


def stage(source, counts, parts):
    (rows, width), rounds = source.shape, counts.shape[0]
    size = counts.shape[2] // parts
    tile = min(128, rows)

    def body(src_ref, counts_ref, copy_ref, low_ref, *weight_refs):
        copy_ref[...] = src_ref[...]
        low_ref[...] = src_ref[...].astype(jnp.bfloat16)
        for index, weight_ref in enumerate(weight_refs):
            turn, part = divmod(index, parts)
            weight_ref[...] = (
                counts_ref[turn, :, part * size : (part + 1) * size].astype(jnp.int8)
            )

    src_spec = pl.BlockSpec((tile, width), lambda i: (i, 0))
    weight_spec = pl.BlockSpec((tile, size), lambda i: (i, 0))
    src_t, src_low_t, _, _, _ = shapes_for(rows, size, width)
    weight_t = jax.ShapeDtypeStruct((rows, size), jnp.int8)
    return pl.pallas_call(
        body,
        grid=(rows // tile,),
        in_specs=[src_spec, pl.BlockSpec((rounds, tile, parts * size), lambda i: (0, i, 0))],
        out_specs=[src_spec, src_spec] + [weight_spec] * (rounds * parts),
        out_shape=[src_t, src_low_t] + [weight_t] * (rounds * parts),
        compiler_params=pltpu.CompilerParams(
            dimension_semantics=("arbitrary",), vmem_limit_bytes=8 * 1024 * 1024
        ),
        cost_estimate=pl.CostEstimate(
            flops=rounds * rows * size * parts,
            bytes_accessed=6 * rounds * rows * size * parts + 10 * rows * width,
            transcendentals=0,
        ),
    )(source, counts)


def join(part_a, part_b):
    size, width = part_a.shape

    def body(a_ref, b_ref, out_ref, arrived):
        copies = [
            pltpu.make_async_copy(a_ref, out_ref.at[pl.ds(0, size)], arrived.at[0]),
            pltpu.make_async_copy(b_ref, out_ref.at[pl.ds(size, size)], arrived.at[1]),
        ]
        for copy in copies:
            copy.start()
        for copy in copies:
            copy.wait()

    return pl.pallas_call(
        body,
        in_specs=[pl.BlockSpec(memory_space=pltpu.VMEM)] * 2,
        out_specs=pl.BlockSpec(memory_space=pltpu.HBM),
        out_shape=jax.ShapeDtypeStruct((2 * size, width), jnp.float32),
        scratch_shapes=[pltpu.SemaphoreType.DMA((2,))],
        compiler_params=pltpu.CompilerParams(vmem_limit_bytes=4 * 1024 * 1024),
    )(part_a, part_b)


def train_early(src_low, ctx, weight):
    (rows, width), size = src_low.shape, ctx.shape[0]
    _, _, ctx_t, coef_t, low_t = shapes_for(rows, size, width)

    def body(src_ref, ctx_ref, weight_ref, new_ctx_ref, coef_out, low_out, coef_ref, low_ref, grad_ref, left):
        low_copy = pltpu.make_async_copy(low_ref, low_out, left.at[0])
        coef_copy = pltpu.make_async_copy(coef_ref, coef_out, left.at[1])
        round_ctx(INNER_TILES, ctx_ref, low_ref, grad_ref)
        low_copy.start()
        early_tiles(INNER_TILES, src_ref, weight_ref, coef_ref, low_ref, grad_ref)
        coef_copy.start()
        update_ctx(INNER_TILES, ctx_ref, grad_ref, new_ctx_ref)
        low_copy.wait()
        coef_copy.wait()

    scratch = [
        pltpu.VMEM((rows, size), jnp.bfloat16),
        pltpu.VMEM((size, width), jnp.bfloat16),
        pltpu.VMEM((size, width), jnp.float32),
        pltpu.SemaphoreType.DMA((2,)),
    ]
    return launch(body, [src_low, ctx, weight], [ctx_t, coef_t, low_t], scratch, rows, size, width, 1, kept=1)


def train_last(tiles, src, ctx, weight, earlier, want_low):
    (rows, width), size = src.shape, ctx.shape[0]
    src_t, src_low_t, ctx_t, _, _ = shapes_for(rows, size, width)

    def body(src_ref, ctx_ref, weight_ref, *refs):
        refs = list(refs)
        early_refs = [refs.pop(0) for _ in earlier]
        new_src_ref = refs.pop(0)
        src_low_ref = refs.pop(0) if want_low else None
        last_part(tiles, src_ref, ctx_ref, weight_ref, early_refs, new_src_ref, src_low_ref, *refs)

    scratch = [pltpu.VMEM((size, width), jnp.bfloat16), pltpu.VMEM((size, width), jnp.float32)]
    outs = [src_t] + ([src_low_t] if want_low else []) + [ctx_t]
    return launch(body, [src, ctx, weight, *earlier], outs, scratch, rows, size, width, 1)


def train_seam(src, ctx_b, weight_b, earlier, ctx_a, weight_a):
    (rows, width), size = src.shape, ctx_a.shape[0]
    src_t, src_low_t, ctx_t, coef_t, low_t = shapes_for(rows, size, width)

    def body(src_ref, b_ref, weight_b_ref, coef_in, low_in, a_ref, weight_a_ref,
             new_src_ref, new_b_ref, new_a_ref, coef_ref, low_ref, src_low_ref, low_b_ref, grad_ref):
        last_part(OUTER_TILES, src_ref, b_ref, weight_b_ref, [coef_in, low_in], new_src_ref, src_low_ref, new_b_ref, low_b_ref, grad_ref)
        early_part(OUTER_TILES, src_low_ref, a_ref, weight_a_ref, new_a_ref, coef_ref, low_ref, grad_ref)

    scratch = [
        pltpu.VMEM((rows, width), jnp.bfloat16),
        pltpu.VMEM((size, width), jnp.bfloat16),
        pltpu.VMEM((size, width), jnp.float32),
    ]
    outs = [src_t, ctx_t, ctx_t, coef_t, low_t]
    return launch(body, [src, ctx_b, weight_b, *earlier, ctx_a, weight_a], outs, scratch, rows, size, width, 2)


def col_move(block, offset, back=False, may_stay=False):
    count = lax.axis_size("col")
    branches = [
        functools.partial(shifted, axis="col", by=step if back else count - step)
        for step in range(1, count)
    ]
    if may_stay:
        return lax.switch(offset, [lambda value: value] + branches, block)
    return lax.switch(offset - 1, branches, block)


def col_hop(block, index):
    count = lax.axis_size("col")
    return lax.switch(
        index, [functools.partial(shifted, axis="col", by=count - step) for step in range(1, count)], block
    )


def row_move(block, offset, back=False, may_stay=False):
    count = lax.axis_size("row")
    branches = [
        functools.partial(shifted, axis="row", by=step if back else count - step)
        for step in range(1, count)
    ]
    if may_stay:
        return lax.switch(offset, [lambda value: value] + branches, block)
    return lax.switch(offset - 1, branches, block)


def totals(partner_masks, rounds):
    row_count = lax.axis_size("row")
    col_count = lax.axis_size("col")
    row_total, col_total = partner_masks[0], partner_masks[1]
    for turn in range(2, rounds, 2):
        row_total = row_total + partner_masks[turn]
        row_total = jnp.where(row_total >= row_count, row_total - row_count, row_total)
        col_total = col_total + partner_masks[turn + 1]
        col_total = jnp.where(col_total >= col_count, col_total - col_count, col_total)
    return row_total, col_total


def per_device_plain(source, context, pair_counts, partner_masks):
    rounds = pair_counts.shape[0]
    for turn in range(rounds):
        move = row_move if turn % 2 == 0 else col_move
        context = move(context, partner_masks[turn])
        source, context = train_last(OUTER_TILES, source, context, pair_counts[turn], [], False)
    row_total, col_total = totals(partner_masks, rounds)
    context = row_move(context, row_total, back=True, may_stay=True)
    return source, col_move(context, col_total, back=True, may_stay=True)


def per_device(source, context, pair_counts, partner_masks):
    rounds = pair_counts.shape[0]
    row_count = lax.axis_size("row")
    col_count = lax.axis_size("col")
    size = context.shape[0] // PARTS

    def opening(by, src, counts, ctx, masks):
        part_a = shifted(ctx[:size], "row", by)
        part_b = shifted(ctx[size:], "row", by)
        hops = [masks[turn] - 1 for turn in range(rounds)]
        src, src_low, *weights = stage(src, counts, PARTS)
        part_a, *early = train_early(src_low, part_a, weights[0])
        part_a = col_hop(part_a, hops[1])
        return src, weights[1:], early, part_a, part_b, totals(masks, rounds), hops

    def middle(by, src, early, part_a, part_b, weights, hop_b, hop_a):
        part_a = shifted(part_a, "row", by)
        part_b = col_hop(part_b, hop_b)
        src, src_low, part_b = train_last(INNER_TILES, src, part_b, weights[0], early, True)
        part_b = shifted(part_b, "row", by)
        part_a, *early = train_early(src_low, part_a, weights[1])
        part_a = col_hop(part_a, hop_a)
        return src, early, part_a, part_b

    src, weights, early, part_a, part_b, (row_total, col_total), hops = lax.switch(
        (partner_masks - 1)[0],
        [functools.partial(opening, row_count - step) for step in range(1, row_count)],
        source, pair_counts, context, partner_masks,
    )
    weights = [None] + list(weights)
    src, part_b, part_a, *early = train_seam(src, part_b, weights[1], early, part_a, weights[2])
    for turn in range(2, rounds, 2):
        here = PARTS * turn
        src, early, part_a, part_b = lax.switch(
            hops[turn],
            [functools.partial(middle, row_count - step) for step in range(1, row_count)],
            src, early, part_a, part_b, weights[here - 1 : here + 1], hops[turn - 1], hops[turn + 1],
        )
        src, part_b, part_a, *early = train_seam(
            src, part_b, weights[here + 1], early, part_a, weights[here + 2]
        )

    def returning(by_row, part_a, part_b):
        part_a = shifted(part_a, "row", by_row) if by_row else part_a
        return part_a, col_hop(part_b, hops[rounds - 1])

    part_a, part_b = lax.switch(
        row_total, [functools.partial(returning, step) for step in range(row_count)], part_a, part_b
    )
    src, part_b = train_last(OUTER_TILES, src, part_b, weights[-1], early, False)

    def closing(by_col, part_a, part_b):
        part_a = shifted(part_a, "col", by_col) if by_col else part_a
        homeward = [
            functools.partial(shifted_both, by_row=by_row, by_col=by_col)
            if by_row or by_col
            else (lambda value: value)
            for by_row in range(row_count)
        ]
        return part_a, lax.switch(row_total, homeward, part_b)

    part_a, part_b = lax.switch(
        col_total, [functools.partial(closing, step) for step in range(col_count)], part_a, part_b
    )
    return src, join(part_a, part_b)


def solution(mesh):
    in_specs = (
        P(("row", "col"), None),
        P(("row", "col"), None),
        P(None, ("row", "col"), None),
        P(),
    )
    out_specs = (P(("row", "col"), None), P(("row", "col"), None))
    few = mesh.shape["row"] * mesh.shape["col"] <= NESTED_LIMIT
    return jax.shard_map(
        per_device if few else per_device_plain, mesh=mesh, in_specs=in_specs, out_specs=out_specs, check_vma=False
    )
```

```python
import functools

import jax
import jax.numpy as jnp
from jax import lax
from jax.experimental import pallas as pl
from jax.experimental.pallas import tpu as pltpu
from jax.sharding import PartitionSpec as P

LEARN_RATE = 0.05
NEG_WEIGHT = 1.0
EPSILON = 1e-06
PARTS = 2
INNER_TILES = 2
EARLY_TILES = 1
OUTER_TILES = 1
CTX_TILES = 2
EARLY_CTX_TILES = 4
NESTED_LIMIT = 32


def shifted(value, axis, by):
    length = lax.axis_size(axis)
    return lax.ppermute(value, axis, [(i, (i + by) % length) for i in range(length)])


def shifted_both(value, by_row, by_col):
    rows, cols = lax.axis_size("row"), lax.axis_size("col")
    pairs = [
        (r * cols + c, (r + by_row) % rows * cols + (c + by_col) % cols)
        for r in range(rows)
        for c in range(cols)
    ]
    return lax.ppermute(value, ("row", "col"), pairs)


def normalized(param, grad):
    scale = lax.rsqrt(jnp.mean(grad * grad, axis=1, keepdims=True) + EPSILON)
    return param - LEARN_RATE * grad * scale


def tiles_of(rows, tiles, body):
    tile = rows // tiles
    if tiles == 1:
        body(pl.ds(0, rows))
        return

    def step(index, carry):
        body(pl.ds(pl.multiple_of(index * tile, tile), tile))
        return carry

    lax.fori_loop(0, tiles, step, 0)


def couple(tiles, src_low, ctx_low, weight_ref, here, grad_ctx_ref):
    scores = lax.dot_general(
        src_low, ctx_low, (((1,), (1,)), ((), ())), preferred_element_type=jnp.float32
    )
    weight = weight_ref[here, :].astype(jnp.int32).astype(jnp.float32)
    coef = ((weight + NEG_WEIGHT) * jax.nn.sigmoid(scores) - weight).astype(jnp.bfloat16)
    grad_ctx = lax.dot_general(
        coef, src_low, (((0,), (0,)), ((), ())), preferred_element_type=jnp.float32
    )
    if tiles == 1:
        grad_ctx_ref[...] = grad_ctx
    else:
        grad_ctx_ref[...] += grad_ctx
    return coef


def round_ctx(tiles, ctx_tiles, ctx_ref, low_ref, grad_ctx_ref):
    def body(here):
        ctx = ctx_ref[here, :]
        low_ref[here, :] = ctx.astype(jnp.bfloat16)
        if tiles > 1:
            grad_ctx_ref[here, :] = jnp.zeros_like(ctx)

    tiles_of(ctx_ref.shape[0], ctx_tiles, body)


def update_ctx(ctx_tiles, ctx_ref, grad_ctx_ref, new_ctx_ref):
    def body(here):
        new_ctx_ref[here, :] = normalized(ctx_ref[here, :], grad_ctx_ref[here, :])

    tiles_of(ctx_ref.shape[0], ctx_tiles, body)


def early_tiles(tiles, src_ref, weight_ref, coef_ref, low_ref, grad_ctx_ref):
    def body(here):
        coef_ref[here, :] = couple(tiles, src_ref[here, :], low_ref[...], weight_ref, here, grad_ctx_ref)

    tiles_of(src_ref.shape[0], tiles, body)


def early_part(tiles, src_ref, ctx_ref, weight_ref, new_ctx_ref, coef_ref, low_ref, grad_ctx_ref):
    ctx_tiles = CTX_TILES if tiles > 1 else 1
    round_ctx(tiles, ctx_tiles, ctx_ref, low_ref, grad_ctx_ref)
    early_tiles(tiles, src_ref, weight_ref, coef_ref, low_ref, grad_ctx_ref)
    update_ctx(ctx_tiles, ctx_ref, grad_ctx_ref, new_ctx_ref)


def last_part(tiles, src_ref, ctx_ref, weight_ref, earlier, new_src_ref, src_low_ref, new_ctx_ref, low_ref, grad_ctx_ref):
    ctx_tiles = CTX_TILES if tiles > 1 else 1
    round_ctx(tiles, ctx_tiles, ctx_ref, low_ref, grad_ctx_ref)

    def body(here):
        src = src_ref[here, :]
        ctx_low = low_ref[...]
        coef = couple(tiles, src.astype(jnp.bfloat16), ctx_low, weight_ref, here, grad_ctx_ref)
        grad_src = jnp.dot(coef, ctx_low, preferred_element_type=jnp.float32)
        if earlier:
            coef_ref, early_ref = earlier
            grad_src = grad_src + jnp.dot(
                coef_ref[here, :], early_ref[...], preferred_element_type=jnp.float32
            )
        new_src = normalized(src, grad_src)
        new_src_ref[here, :] = new_src
        if src_low_ref is not None:
            src_low_ref[here, :] = new_src.astype(jnp.bfloat16)

    tiles_of(src_ref.shape[0], tiles, body)
    update_ctx(ctx_tiles, ctx_ref, grad_ctx_ref, new_ctx_ref)


def launch(body, operands, out_shape, scratch_shapes, rows, size, width, pieces, kept=None):
    whole = pl.BlockSpec(memory_space=pltpu.VMEM)
    kept = len(out_shape) if kept is None else kept
    return pl.pallas_call(
        body,
        in_specs=[whole] * len(operands),
        out_specs=[whole] * kept + [pl.BlockSpec(memory_space=pl.ANY)] * (len(out_shape) - kept),
        out_shape=out_shape,
        scratch_shapes=scratch_shapes,
        compiler_params=pltpu.CompilerParams(vmem_limit_bytes=12 * 1024 * 1024),
        cost_estimate=pl.CostEstimate(
            flops=6 * rows * size * width * pieces,
            bytes_accessed=4 * (2 * rows * width + pieces * (2 * size * width + rows * size)),
            transcendentals=rows * size * pieces,
        ),
    )(*operands)


def shapes_for(rows, size, width):
    src = jax.ShapeDtypeStruct((rows, width), jnp.float32)
    src_low = jax.ShapeDtypeStruct((rows, width), jnp.bfloat16)
    ctx = jax.ShapeDtypeStruct((size, width), jnp.float32)
    coef = jax.ShapeDtypeStruct((rows, size), jnp.bfloat16)
    low = jax.ShapeDtypeStruct((size, width), jnp.bfloat16)
    return src, src_low, ctx, coef, low


def stage(source, counts, parts):
    (rows, width), rounds = source.shape, counts.shape[0]
    size = counts.shape[2] // parts
    tile = min(128, rows)

    def body(src_ref, counts_ref, copy_ref, low_ref, *weight_refs):
        copy_ref[...] = src_ref[...]
        low_ref[...] = src_ref[...].astype(jnp.bfloat16)
        for index, weight_ref in enumerate(weight_refs):
            turn, part = divmod(index, parts)
            weight_ref[...] = (
                counts_ref[turn, :, part * size : (part + 1) * size].astype(jnp.int8)
            )

    src_spec = pl.BlockSpec((tile, width), lambda i: (i, 0))
    weight_spec = pl.BlockSpec((tile, size), lambda i: (i, 0))
    src_t, src_low_t, _, _, _ = shapes_for(rows, size, width)
    weight_t = jax.ShapeDtypeStruct((rows, size), jnp.int8)
    return pl.pallas_call(
        body,
        grid=(rows // tile,),
        in_specs=[src_spec, pl.BlockSpec((rounds, tile, parts * size), lambda i: (0, i, 0))],
        out_specs=[src_spec, src_spec] + [weight_spec] * (rounds * parts),
        out_shape=[src_t, src_low_t] + [weight_t] * (rounds * parts),
        compiler_params=pltpu.CompilerParams(
            dimension_semantics=("arbitrary",), vmem_limit_bytes=8 * 1024 * 1024
        ),
        cost_estimate=pl.CostEstimate(
            flops=rounds * rows * size * parts,
            bytes_accessed=6 * rounds * rows * size * parts + 10 * rows * width,
            transcendentals=0,
        ),
    )(source, counts)


def join(part_a, part_b):
    size, width = part_a.shape

    def body(a_ref, b_ref, out_ref, arrived):
        copies = [
            pltpu.make_async_copy(a_ref, out_ref.at[pl.ds(0, size)], arrived.at[0]),
            pltpu.make_async_copy(b_ref, out_ref.at[pl.ds(size, size)], arrived.at[1]),
        ]
        for copy in copies:
            copy.start()
        for copy in copies:
            copy.wait()

    return pl.pallas_call(
        body,
        in_specs=[pl.BlockSpec(memory_space=pltpu.VMEM)] * 2,
        out_specs=pl.BlockSpec(memory_space=pltpu.HBM),
        out_shape=jax.ShapeDtypeStruct((2 * size, width), jnp.float32),
        scratch_shapes=[pltpu.SemaphoreType.DMA((2,))],
        compiler_params=pltpu.CompilerParams(vmem_limit_bytes=4 * 1024 * 1024),
    )(part_a, part_b)


def train_early(src_low, ctx, weight):
    (rows, width), size = src_low.shape, ctx.shape[0]
    _, _, ctx_t, coef_t, low_t = shapes_for(rows, size, width)

    def body(src_ref, ctx_ref, weight_ref, new_ctx_ref, coef_out, low_out, coef_ref, low_ref, grad_ref, left):
        low_copy = pltpu.make_async_copy(low_ref, low_out, left.at[0])
        coef_copy = pltpu.make_async_copy(coef_ref, coef_out, left.at[1])
        round_ctx(EARLY_TILES, EARLY_CTX_TILES, ctx_ref, low_ref, grad_ref)
        low_copy.start()
        early_tiles(EARLY_TILES, src_ref, weight_ref, coef_ref, low_ref, grad_ref)
        coef_copy.start()
        update_ctx(EARLY_CTX_TILES, ctx_ref, grad_ref, new_ctx_ref)
        low_copy.wait()
        coef_copy.wait()

    scratch = [
        pltpu.VMEM((rows, size), jnp.bfloat16),
        pltpu.VMEM((size, width), jnp.bfloat16),
        pltpu.VMEM((size, width), jnp.float32),
        pltpu.SemaphoreType.DMA((2,)),
    ]
    return launch(body, [src_low, ctx, weight], [ctx_t, coef_t, low_t], scratch, rows, size, width, 1, kept=1)


def train_last(tiles, src, ctx, weight, earlier, want_low):
    (rows, width), size = src.shape, ctx.shape[0]
    src_t, src_low_t, ctx_t, _, _ = shapes_for(rows, size, width)

    def body(src_ref, ctx_ref, weight_ref, *refs):
        refs = list(refs)
        early_refs = [refs.pop(0) for _ in earlier]
        new_src_ref = refs.pop(0)
        src_low_ref = refs.pop(0) if want_low else None
        last_part(tiles, src_ref, ctx_ref, weight_ref, early_refs, new_src_ref, src_low_ref, *refs)

    scratch = [pltpu.VMEM((size, width), jnp.bfloat16), pltpu.VMEM((size, width), jnp.float32)]
    outs = [src_t] + ([src_low_t] if want_low else []) + [ctx_t]
    return launch(body, [src, ctx, weight, *earlier], outs, scratch, rows, size, width, 1)


def train_seam(src, ctx_b, weight_b, earlier, ctx_a, weight_a):
    (rows, width), size = src.shape, ctx_a.shape[0]
    src_t, src_low_t, ctx_t, coef_t, low_t = shapes_for(rows, size, width)

    def body(src_ref, b_ref, weight_b_ref, coef_in, low_in, a_ref, weight_a_ref,
             new_src_ref, new_b_ref, new_a_ref, coef_ref, low_ref, src_low_ref, low_b_ref, grad_ref):
        last_part(OUTER_TILES, src_ref, b_ref, weight_b_ref, [coef_in, low_in], new_src_ref, src_low_ref, new_b_ref, low_b_ref, grad_ref)
        early_part(OUTER_TILES, src_low_ref, a_ref, weight_a_ref, new_a_ref, coef_ref, low_ref, grad_ref)

    scratch = [
        pltpu.VMEM((rows, width), jnp.bfloat16),
        pltpu.VMEM((size, width), jnp.bfloat16),
        pltpu.VMEM((size, width), jnp.float32),
    ]
    outs = [src_t, ctx_t, ctx_t, coef_t, low_t]
    return launch(body, [src, ctx_b, weight_b, *earlier, ctx_a, weight_a], outs, scratch, rows, size, width, 2)


def col_move(block, offset, back=False, may_stay=False):
    count = lax.axis_size("col")
    branches = [
        functools.partial(shifted, axis="col", by=step if back else count - step)
        for step in range(1, count)
    ]
    if may_stay:
        return lax.switch(offset, [lambda value: value] + branches, block)
    return lax.switch(offset - 1, branches, block)


def col_hop(block, index):
    count = lax.axis_size("col")
    return lax.switch(
        index, [functools.partial(shifted, axis="col", by=count - step) for step in range(1, count)], block
    )


def row_move(block, offset, back=False, may_stay=False):
    count = lax.axis_size("row")
    branches = [
        functools.partial(shifted, axis="row", by=step if back else count - step)
        for step in range(1, count)
    ]
    if may_stay:
        return lax.switch(offset, [lambda value: value] + branches, block)
    return lax.switch(offset - 1, branches, block)


def totals(partner_masks, rounds):
    row_count = lax.axis_size("row")
    col_count = lax.axis_size("col")
    row_total, col_total = partner_masks[0], partner_masks[1]
    for turn in range(2, rounds, 2):
        row_total = row_total + partner_masks[turn]
        row_total = jnp.where(row_total >= row_count, row_total - row_count, row_total)
        col_total = col_total + partner_masks[turn + 1]
        col_total = jnp.where(col_total >= col_count, col_total - col_count, col_total)
    return row_total, col_total


def per_device_plain(source, context, pair_counts, partner_masks):
    rounds = pair_counts.shape[0]
    for turn in range(rounds):
        move = row_move if turn % 2 == 0 else col_move
        context = move(context, partner_masks[turn])
        source, context = train_last(OUTER_TILES, source, context, pair_counts[turn], [], False)
    row_total, col_total = totals(partner_masks, rounds)
    context = row_move(context, row_total, back=True, may_stay=True)
    return source, col_move(context, col_total, back=True, may_stay=True)


def per_device(source, context, pair_counts, partner_masks):
    rounds = pair_counts.shape[0]
    row_count = lax.axis_size("row")
    col_count = lax.axis_size("col")
    size = context.shape[0] // PARTS

    def opening(by, src, counts, ctx, masks):
        part_a, ctx = lax.optimization_barrier((ctx[:size], ctx))
        part_a = shifted(part_a, "row", by)
        part_b = shifted(ctx[size:], "row", by)
        hops = [masks[turn] - 1 for turn in range(rounds)]
        src, src_low, *weights = stage(src, counts, PARTS)
        part_a, *early = train_early(src_low, part_a, weights[0])
        part_a = col_hop(part_a, hops[1])
        return src, weights[1:], early, part_a, part_b, totals(masks, rounds), hops

    def middle(by, src, early, part_a, part_b, weights, hop_b, hop_a):
        part_a = shifted(part_a, "row", by)
        part_b = col_hop(part_b, hop_b)
        src, src_low, part_b = train_last(INNER_TILES, src, part_b, weights[0], early, True)
        part_b = shifted(part_b, "row", by)
        part_a, *early = train_early(src_low, part_a, weights[1])
        part_a = col_hop(part_a, hop_a)
        return src, early, part_a, part_b

    src, weights, early, part_a, part_b, (row_total, col_total), hops = lax.switch(
        (partner_masks - 1)[0],
        [functools.partial(opening, row_count - step) for step in range(1, row_count)],
        source, pair_counts, context, partner_masks,
    )
    weights = [None] + list(weights)
    src, part_b, part_a, *early = train_seam(src, part_b, weights[1], early, part_a, weights[2])
    for turn in range(2, rounds, 2):
        here = PARTS * turn
        src, early, part_a, part_b = lax.switch(
            hops[turn],
            [functools.partial(middle, row_count - step) for step in range(1, row_count)],
            src, early, part_a, part_b, weights[here - 1 : here + 1], hops[turn - 1], hops[turn + 1],
        )
        src, part_b, part_a, *early = train_seam(
            src, part_b, weights[here + 1], early, part_a, weights[here + 2]
        )

    def returning(by_row, part_a, part_b):
        part_a = shifted(part_a, "row", by_row) if by_row else part_a
        return part_a, col_hop(part_b, hops[rounds - 1])

    part_a, part_b = lax.switch(
        row_total, [functools.partial(returning, step) for step in range(row_count)], part_a, part_b
    )
    src, part_b = train_last(OUTER_TILES, src, part_b, weights[-1], early, False)

    def closing(by_col, part_a, part_b):
        part_a = shifted(part_a, "col", by_col) if by_col else part_a
        homeward = [
            functools.partial(shifted_both, by_row=by_row, by_col=by_col)
            if by_row or by_col
            else (lambda value: value)
            for by_row in range(row_count)
        ]
        return join(part_a, lax.switch(row_total, homeward, part_b))

    ctx = lax.switch(
        col_total, [functools.partial(closing, step) for step in range(col_count)], part_a, part_b
    )
    return src, ctx


def solution(mesh):
    in_specs = (
        P(("row", "col"), None),
        P(("row", "col"), None),
        P(None, ("row", "col"), None),
        P(),
    )
    out_specs = (P(("row", "col"), None), P(("row", "col"), None))
    few = mesh.shape["row"] * mesh.shape["col"] <= NESTED_LIMIT
    return jax.shard_map(
        per_device if few else per_device_plain, mesh=mesh, in_specs=in_specs, out_specs=out_specs, check_vma=False
    )
```

```python
import functools

import jax
import jax.numpy as jnp
from jax import lax
from jax.experimental import pallas as pl
from jax.experimental.pallas import tpu as pltpu
from jax.sharding import PartitionSpec as P

LEARN_RATE = 0.05
NEG_WEIGHT = 1.0
EPSILON = 1e-06
PARTS = 2
INNER_TILES = 2
EARLY_TILES = 1
OUTER_TILES = 1
CTX_TILES = 2
EARLY_CTX_TILES = 4
NESTED_LIMIT = 32


def shifted(value, axis, by):
    length = lax.axis_size(axis)
    return lax.ppermute(value, axis, [(i, (i + by) % length) for i in range(length)])


def shifted_both(value, by_row, by_col):
    rows, cols = lax.axis_size("row"), lax.axis_size("col")
    pairs = [
        (r * cols + c, (r + by_row) % rows * cols + (c + by_col) % cols)
        for r in range(rows)
        for c in range(cols)
    ]
    return lax.ppermute(value, ("row", "col"), pairs)


def normalized(param, grad):
    scale = lax.rsqrt(jnp.mean(grad * grad, axis=1, keepdims=True) + EPSILON)
    return param - LEARN_RATE * grad * scale


def tiles_of(rows, tiles, body):
    tile = rows // tiles
    if tiles == 1:
        body(pl.ds(0, rows))
        return

    def step(index, carry):
        body(pl.ds(pl.multiple_of(index * tile, tile), tile))
        return carry

    lax.fori_loop(0, tiles, step, 0)


def couple(tiles, src_low, ctx_low, weight_ref, here, grad_ctx_ref):
    scores = lax.dot_general(
        src_low, ctx_low, (((1,), (1,)), ((), ())), preferred_element_type=jnp.float32
    )
    weight = weight_ref[here, :].astype(jnp.int32).astype(jnp.float32)
    coef = ((weight + NEG_WEIGHT) * jax.nn.sigmoid(scores) - weight).astype(jnp.bfloat16)
    grad_ctx = lax.dot_general(
        coef, src_low, (((0,), (0,)), ((), ())), preferred_element_type=jnp.float32
    )
    if tiles == 1:
        grad_ctx_ref[...] = grad_ctx
    else:
        grad_ctx_ref[...] += grad_ctx
    return coef


def round_ctx(tiles, ctx_tiles, ctx_ref, low_ref, grad_ctx_ref):
    def body(here):
        ctx = ctx_ref[here, :]
        low_ref[here, :] = ctx.astype(jnp.bfloat16)
        if tiles > 1:
            grad_ctx_ref[here, :] = jnp.zeros_like(ctx)

    tiles_of(ctx_ref.shape[0], ctx_tiles, body)


def update_ctx(ctx_tiles, ctx_ref, grad_ctx_ref, new_ctx_ref):
    def body(here):
        new_ctx_ref[here, :] = normalized(ctx_ref[here, :], grad_ctx_ref[here, :])

    tiles_of(ctx_ref.shape[0], ctx_tiles, body)


def early_tiles(tiles, src_ref, weight_ref, coef_ref, low_ref, grad_ctx_ref):
    def body(here):
        coef_ref[here, :] = couple(tiles, src_ref[here, :], low_ref[...], weight_ref, here, grad_ctx_ref)

    tiles_of(src_ref.shape[0], tiles, body)


def early_part(tiles, src_ref, ctx_ref, weight_ref, new_ctx_ref, coef_ref, low_ref, grad_ctx_ref):
    ctx_tiles = CTX_TILES if tiles > 1 else 1
    round_ctx(tiles, ctx_tiles, ctx_ref, low_ref, grad_ctx_ref)
    early_tiles(tiles, src_ref, weight_ref, coef_ref, low_ref, grad_ctx_ref)
    update_ctx(ctx_tiles, ctx_ref, grad_ctx_ref, new_ctx_ref)


def last_part(tiles, src_ref, ctx_ref, weight_ref, earlier, new_src_ref, src_low_ref, new_ctx_ref, low_ref, grad_ctx_ref):
    ctx_tiles = CTX_TILES if tiles > 1 else 1
    round_ctx(tiles, ctx_tiles, ctx_ref, low_ref, grad_ctx_ref)

    def body(here):
        src = src_ref[here, :]
        ctx_low = low_ref[...]
        coef = couple(tiles, src.astype(jnp.bfloat16), ctx_low, weight_ref, here, grad_ctx_ref)
        if earlier:
            coef_ref, early_ref = earlier
            coef = jnp.concatenate([coef_ref[here, :], coef], axis=1)
            ctx_low = jnp.concatenate([early_ref[...], ctx_low], axis=0)
        grad_src = jnp.dot(coef, ctx_low, preferred_element_type=jnp.float32)
        new_src = normalized(src, grad_src)
        new_src_ref[here, :] = new_src
        if src_low_ref is not None:
            src_low_ref[here, :] = new_src.astype(jnp.bfloat16)

    tiles_of(src_ref.shape[0], tiles, body)
    update_ctx(ctx_tiles, ctx_ref, grad_ctx_ref, new_ctx_ref)


def launch(body, operands, out_shape, scratch_shapes, rows, size, width, pieces, kept=None):
    whole = pl.BlockSpec(memory_space=pltpu.VMEM)
    kept = len(out_shape) if kept is None else kept
    return pl.pallas_call(
        body,
        in_specs=[whole] * len(operands),
        out_specs=[whole] * kept + [pl.BlockSpec(memory_space=pl.ANY)] * (len(out_shape) - kept),
        out_shape=out_shape,
        scratch_shapes=scratch_shapes,
        compiler_params=pltpu.CompilerParams(vmem_limit_bytes=12 * 1024 * 1024),
        cost_estimate=pl.CostEstimate(
            flops=6 * rows * size * width * pieces,
            bytes_accessed=4 * (2 * rows * width + pieces * (2 * size * width + rows * size)),
            transcendentals=rows * size * pieces,
        ),
    )(*operands)


def shapes_for(rows, size, width):
    src = jax.ShapeDtypeStruct((rows, width), jnp.float32)
    src_low = jax.ShapeDtypeStruct((rows, width), jnp.bfloat16)
    ctx = jax.ShapeDtypeStruct((size, width), jnp.float32)
    coef = jax.ShapeDtypeStruct((rows, size), jnp.bfloat16)
    low = jax.ShapeDtypeStruct((size, width), jnp.bfloat16)
    return src, src_low, ctx, coef, low


def stage(source, counts, parts):
    (rows, width), rounds = source.shape, counts.shape[0]
    size = counts.shape[2] // parts
    tile = min(128, rows)

    def body(src_ref, counts_ref, copy_ref, low_ref, *weight_refs):
        copy_ref[...] = src_ref[...]
        low_ref[...] = src_ref[...].astype(jnp.bfloat16)
        for index, weight_ref in enumerate(weight_refs):
            turn, part = divmod(index, parts)
            weight_ref[...] = (
                counts_ref[turn, :, part * size : (part + 1) * size].astype(jnp.int8)
            )

    src_spec = pl.BlockSpec((tile, width), lambda i: (i, 0))
    weight_spec = pl.BlockSpec((tile, size), lambda i: (i, 0))
    src_t, src_low_t, _, _, _ = shapes_for(rows, size, width)
    weight_t = jax.ShapeDtypeStruct((rows, size), jnp.int8)
    return pl.pallas_call(
        body,
        grid=(rows // tile,),
        in_specs=[src_spec, pl.BlockSpec((rounds, tile, parts * size), lambda i: (0, i, 0))],
        out_specs=[src_spec, src_spec] + [weight_spec] * (rounds * parts),
        out_shape=[src_t, src_low_t] + [weight_t] * (rounds * parts),
        compiler_params=pltpu.CompilerParams(
            dimension_semantics=("arbitrary",), vmem_limit_bytes=8 * 1024 * 1024
        ),
        cost_estimate=pl.CostEstimate(
            flops=rounds * rows * size * parts,
            bytes_accessed=6 * rounds * rows * size * parts + 10 * rows * width,
            transcendentals=0,
        ),
    )(source, counts)


def join(part_a, part_b):
    size, width = part_a.shape

    def body(a_ref, b_ref, out_ref, arrived):
        copies = [
            pltpu.make_async_copy(a_ref, out_ref.at[pl.ds(0, size)], arrived.at[0]),
            pltpu.make_async_copy(b_ref, out_ref.at[pl.ds(size, size)], arrived.at[1]),
        ]
        for copy in copies:
            copy.start()
        for copy in copies:
            copy.wait()

    return pl.pallas_call(
        body,
        in_specs=[pl.BlockSpec(memory_space=pltpu.VMEM)] * 2,
        out_specs=pl.BlockSpec(memory_space=pltpu.HBM),
        out_shape=jax.ShapeDtypeStruct((2 * size, width), jnp.float32),
        scratch_shapes=[pltpu.SemaphoreType.DMA((2,))],
        compiler_params=pltpu.CompilerParams(vmem_limit_bytes=4 * 1024 * 1024),
    )(part_a, part_b)


def train_early(src_low, ctx, weight):
    (rows, width), size = src_low.shape, ctx.shape[0]
    _, _, ctx_t, coef_t, low_t = shapes_for(rows, size, width)

    def body(src_ref, ctx_ref, weight_ref, new_ctx_ref, coef_out, low_out, coef_ref, low_ref, grad_ref, left):
        low_copy = pltpu.make_async_copy(low_ref, low_out, left.at[0])
        coef_copy = pltpu.make_async_copy(coef_ref, coef_out, left.at[1])
        round_ctx(EARLY_TILES, EARLY_CTX_TILES, ctx_ref, low_ref, grad_ref)
        low_copy.start()
        early_tiles(EARLY_TILES, src_ref, weight_ref, coef_ref, low_ref, grad_ref)
        coef_copy.start()
        update_ctx(EARLY_CTX_TILES, ctx_ref, grad_ref, new_ctx_ref)
        low_copy.wait()
        coef_copy.wait()

    scratch = [
        pltpu.VMEM((rows, size), jnp.bfloat16),
        pltpu.VMEM((size, width), jnp.bfloat16),
        pltpu.VMEM((size, width), jnp.float32),
        pltpu.SemaphoreType.DMA((2,)),
    ]
    return launch(body, [src_low, ctx, weight], [ctx_t, coef_t, low_t], scratch, rows, size, width, 1, kept=1)


def train_last(tiles, src, ctx, weight, earlier, want_low):
    (rows, width), size = src.shape, ctx.shape[0]
    src_t, src_low_t, ctx_t, _, _ = shapes_for(rows, size, width)

    def body(src_ref, ctx_ref, weight_ref, *refs):
        refs = list(refs)
        early_refs = [refs.pop(0) for _ in earlier]
        new_src_ref = refs.pop(0)
        src_low_ref = refs.pop(0) if want_low else None
        last_part(tiles, src_ref, ctx_ref, weight_ref, early_refs, new_src_ref, src_low_ref, *refs)

    scratch = [pltpu.VMEM((size, width), jnp.bfloat16), pltpu.VMEM((size, width), jnp.float32)]
    outs = [src_t] + ([src_low_t] if want_low else []) + [ctx_t]
    return launch(body, [src, ctx, weight, *earlier], outs, scratch, rows, size, width, 1)


def train_seam(src, ctx_b, weight_b, earlier, ctx_a, weight_a):
    (rows, width), size = src.shape, ctx_a.shape[0]
    src_t, src_low_t, ctx_t, coef_t, low_t = shapes_for(rows, size, width)

    def body(src_ref, b_ref, weight_b_ref, coef_in, low_in, a_ref, weight_a_ref,
             new_src_ref, new_b_ref, new_a_ref, coef_ref, low_ref, src_low_ref, low_b_ref, grad_ref):
        last_part(OUTER_TILES, src_ref, b_ref, weight_b_ref, [coef_in, low_in], new_src_ref, src_low_ref, new_b_ref, low_b_ref, grad_ref)
        early_part(OUTER_TILES, src_low_ref, a_ref, weight_a_ref, new_a_ref, coef_ref, low_ref, grad_ref)

    scratch = [
        pltpu.VMEM((rows, width), jnp.bfloat16),
        pltpu.VMEM((size, width), jnp.bfloat16),
        pltpu.VMEM((size, width), jnp.float32),
    ]
    outs = [src_t, ctx_t, ctx_t, coef_t, low_t]
    return launch(body, [src, ctx_b, weight_b, *earlier, ctx_a, weight_a], outs, scratch, rows, size, width, 2)


def col_move(block, offset, back=False, may_stay=False):
    count = lax.axis_size("col")
    branches = [
        functools.partial(shifted, axis="col", by=step if back else count - step)
        for step in range(1, count)
    ]
    if may_stay:
        return lax.switch(offset, [lambda value: value] + branches, block)
    return lax.switch(offset - 1, branches, block)


def col_hop(block, index):
    count = lax.axis_size("col")
    return lax.switch(
        index, [functools.partial(shifted, axis="col", by=count - step) for step in range(1, count)], block
    )


def row_move(block, offset, back=False, may_stay=False):
    count = lax.axis_size("row")
    branches = [
        functools.partial(shifted, axis="row", by=step if back else count - step)
        for step in range(1, count)
    ]
    if may_stay:
        return lax.switch(offset, [lambda value: value] + branches, block)
    return lax.switch(offset - 1, branches, block)


def totals(partner_masks, rounds):
    row_count = lax.axis_size("row")
    col_count = lax.axis_size("col")
    row_total, col_total = partner_masks[0], partner_masks[1]
    for turn in range(2, rounds, 2):
        row_total = row_total + partner_masks[turn]
        row_total = jnp.where(row_total >= row_count, row_total - row_count, row_total)
        col_total = col_total + partner_masks[turn + 1]
        col_total = jnp.where(col_total >= col_count, col_total - col_count, col_total)
    return row_total, col_total


def per_device_plain(source, context, pair_counts, partner_masks):
    rounds = pair_counts.shape[0]
    for turn in range(rounds):
        move = row_move if turn % 2 == 0 else col_move
        context = move(context, partner_masks[turn])
        source, context = train_last(OUTER_TILES, source, context, pair_counts[turn], [], False)
    row_total, col_total = totals(partner_masks, rounds)
    context = row_move(context, row_total, back=True, may_stay=True)
    return source, col_move(context, col_total, back=True, may_stay=True)


def per_device(source, context, pair_counts, partner_masks):
    rounds = pair_counts.shape[0]
    row_count = lax.axis_size("row")
    col_count = lax.axis_size("col")
    size = context.shape[0] // PARTS

    def opening(by, src, counts, ctx, masks):
        part_a, ctx = lax.optimization_barrier((ctx[:size], ctx))
        part_a = shifted(part_a, "row", by)
        part_b = shifted(ctx[size:], "row", by)
        hops = [masks[turn] - 1 for turn in range(rounds)]
        src, src_low, *weights = stage(src, counts, PARTS)
        part_a, *early = train_early(src_low, part_a, weights[0])
        part_a = col_hop(part_a, hops[1])
        return src, weights[1:], early, part_a, part_b, totals(masks, rounds), hops

    def middle(by, src, early, part_a, part_b, weights, hop_b, hop_a):
        part_a = shifted(part_a, "row", by)
        part_b = col_hop(part_b, hop_b)
        src, src_low, part_b = train_last(INNER_TILES, src, part_b, weights[0], early, True)
        part_b = shifted(part_b, "row", by)
        part_a, *early = train_early(src_low, part_a, weights[1])
        part_a = col_hop(part_a, hop_a)
        return src, early, part_a, part_b

    src, weights, early, part_a, part_b, (row_total, col_total), hops = lax.switch(
        (partner_masks - 1)[0],
        [functools.partial(opening, row_count - step) for step in range(1, row_count)],
        source, pair_counts, context, partner_masks,
    )
    weights = [None] + list(weights)
    src, part_b, part_a, *early = train_seam(src, part_b, weights[1], early, part_a, weights[2])
    for turn in range(2, rounds, 2):
        here = PARTS * turn
        src, early, part_a, part_b = lax.switch(
            hops[turn],
            [functools.partial(middle, row_count - step) for step in range(1, row_count)],
            src, early, part_a, part_b, weights[here - 1 : here + 1], hops[turn - 1], hops[turn + 1],
        )
        src, part_b, part_a, *early = train_seam(
            src, part_b, weights[here + 1], early, part_a, weights[here + 2]
        )

    def returning(by_row, part_a, part_b):
        part_a = shifted(part_a, "row", by_row) if by_row else part_a
        return part_a, col_hop(part_b, hops[rounds - 1])

    part_a, part_b = lax.switch(
        row_total, [functools.partial(returning, step) for step in range(row_count)], part_a, part_b
    )
    src, part_b = train_last(OUTER_TILES, src, part_b, weights[-1], early, False)

    def closing(by_col, part_a, part_b):
        part_a = shifted(part_a, "col", by_col) if by_col else part_a
        homeward = [
            functools.partial(shifted_both, by_row=by_row, by_col=by_col)
            if by_row or by_col
            else (lambda value: value)
            for by_row in range(row_count)
        ]
        return join(part_a, lax.switch(row_total, homeward, part_b))

    ctx = lax.switch(
        col_total, [functools.partial(closing, step) for step in range(col_count)], part_a, part_b
    )
    return src, ctx


def solution(mesh):
    in_specs = (
        P(("row", "col"), None),
        P(("row", "col"), None),
        P(None, ("row", "col"), None),
        P(),
    )
    out_specs = (P(("row", "col"), None), P(("row", "col"), None))
    few = mesh.shape["row"] * mesh.shape["col"] <= NESTED_LIMIT
    return jax.shard_map(
        per_device if few else per_device_plain, mesh=mesh, in_specs=in_specs, out_specs=out_specs, check_vma=False
    )
```
